256 devices in a mesh: seq: 8 (over y, core), vocab: 32 (over z, x).
Axes of the slice: x: 4, y: 4, z: 8, core: 2. Of those that a mesh axis runs over, the one named last changes fastest.
Arguments:
- hidden: bfloat16 [2, 1024, 5120], P(None, 'seq'), may hold values from -128 to 128
- head_weight: bfloat16 [5120, 77824], P('seq', 'vocab'), may hold values from -1 to 1
- ref_logits: bfloat16 [2, 1024, 77824], P(None, 'seq', 'vocab'), may hold values from -320 to 320
- token_ids: int32 [2, 1024], P(None, 'seq'), may hold values from 0 to 77823
- end_pos: int32 [2], replicated, may hold values from 512 to 1023
- loss_mask: int32 [2, 1024], P(None, 'seq'), may hold values 0 or 1
- scores: float32 [2], replicated, may hold values from -8 to 8
Outputs:
- logit_grad: bfloat16 [2, 1024, 77824], P(None, 'seq', 'vocab')
- hidden_grad: bfloat16 [2, 1024, 5120], P(None, 'seq', 'vocab')
- advantages: float32 [2, 1024], P(None, 'seq')
The draws below stay inside these ranges and needn't reach their ends.
All inputs are finite; a program needn't handle non-finite values. No bound on the sum of `loss_mask` on one device may be relied on, other than what follows from the above.
Results may differ from the reference program's by a relative error of at most 0.0039.
The reference program's roundings to bfloat16 on the way count: a program that leaves them out, or rounds other values in their place, can miss the bound.
Values may be sent and summed in bfloat16 or wider, within the bound.
No kernel may reach another device: no remote copies, remote signals or barrier semaphores. Data moves between devices by JAX's collectives and lax.ppermute only.
A program may use at most 128 MiB of HBM per device.

```python
import math
import jax
import jax.numpy as jnp
from jax import lax

D = 5120
VOCAB = 77824
BATCH = 2
SEQ_LEN = 1024


HIDDEN_LIMIT = 128.0


def special_columns(key):
    base = jax.random.fold_in(key, 77)
    keys = jax.random.split(base, 4)
    first_index = jax.random.randint(keys[0], (), 0, VOCAB)
    second_index = (first_index + 1 + jax.random.randint(keys[1], (), 0, VOCAB - 1)) % VOCAB
    first_col = jax.random.normal(keys[2], (D,), jnp.float32) / math.sqrt(D)
    second_col = jax.random.normal(keys[3], (D,), jnp.float32) / math.sqrt(D)
    second_col = second_col - jnp.dot(second_col, first_col) / jnp.dot(first_col, first_col) * first_col
    return (first_index, second_index, first_col, second_col)


def head_column(key, column_index, specials):
    first_index, second_index, first_col, second_col = specials
    column = jax.random.normal(jax.random.fold_in(jax.random.fold_in(key, 5), column_index), (D,), jnp.float32)
    column = jnp.clip(column, -6.0, 6.0) / math.sqrt(D)
    column = jnp.where(column_index == first_index, first_col, column)
    return jnp.where(column_index == second_index, second_col, column)


def token_draw(key):
    return jax.random.randint(jax.random.fold_in(key, 31), (BATCH, SEQ_LEN), 0, VOCAB).astype(jnp.int32)


def draw_token_ids(key, part):
    return token_draw(key)


def draw_head_weight(key, part):
    specials = special_columns(key)
    columns = jax.vmap(lambda column_index: head_column(key, column_index, specials))(jnp.arange(VOCAB).astype(jnp.int32))
    return jnp.transpose(columns).astype(jnp.bfloat16)


def draw_hidden(key, part):
    states = 3.0 * jnp.clip(jax.random.normal(jax.random.fold_in(key, 6), (BATCH, SEQ_LEN, D), jnp.float32), -6.0, 6.0)
    specials = special_columns(key)
    tokens = token_draw(key).reshape(BATCH * SEQ_LEN)
    token_columns = jax.vmap(lambda column_index: head_column(key, column_index, specials))(tokens)
    token_columns = token_columns.reshape(BATCH, SEQ_LEN, D)
    boost_size = jax.random.uniform(jax.random.fold_in(key, 10), (BATCH, SEQ_LEN, 1), jnp.float32, 6.0, 19.0)
    states = states + boost_size * token_columns / jnp.sum(token_columns * token_columns, axis=2, keepdims=True)
    states = jnp.clip(states, -HIDDEN_LIMIT, HIDDEN_LIMIT)
    return states.astype(jnp.bfloat16)


def draw_ref_logits(key, part):
    values = 1.5 * jnp.clip(jax.random.normal(jax.random.fold_in(key, 21), (BATCH, SEQ_LEN, VOCAB), jnp.float32), -6.0, 6.0)
    return values.astype(jnp.bfloat16)


def with_ends(values, stream_key, low, top_value):
    shape = values.shape
    spot = [jax.random.randint(jax.random.fold_in(stream_key, axis), (), 0, shape[axis]) for axis in range(len(shape))]
    values = values.at[tuple(spot)].set(low)
    longest = shape.index(max(shape))
    spot[longest] = (spot[longest] + 1) % shape[longest]
    return values.at[tuple(spot)].set(top_value)


def centred(own_key, extent, scale, bound, held_as=jnp.bfloat16):
    result = scale * jax.random.normal(own_key, extent, jnp.float32)
    return jnp.clip(result, min=-bound, max=bound).astype(held_as)


def setup_inputs(seed: int = 0) -> dict:
    splits = jax.random.split(jax.random.key(seed), 8)
    return {
        "hidden": draw_hidden(jax.random.fold_in(splits[7], 71), 0),
        "head_weight": draw_head_weight(jax.random.fold_in(splits[7], 71), 0),
        "ref_logits": draw_ref_logits(jax.random.fold_in(splits[7], 71), 0),
        "token_ids": draw_token_ids(jax.random.fold_in(splits[7], 71), 0),
        "end_pos": jax.random.randint(splits[4], (BATCH,), SEQ_LEN // 2, SEQ_LEN).astype(jnp.int32),
        "loss_mask": with_ends((jax.random.randint(splits[5], (BATCH, SEQ_LEN), 0, 4) < 3).astype(jnp.int32), jax.random.fold_in(splits[5], 1), 0, 1),
        "scores": centred(splits[6], (BATCH,), 2.0, 8.0, jnp.float32),
    }


def row_stats(pair, head_weight):
    states, refs = pair
    logits = jnp.dot(states, head_weight, preferred_element_type=jnp.float32)
    refs = refs.astype(jnp.float32)
    top_policy = lax.optimization_barrier(jnp.max(logits, axis=1))
    expo = jnp.exp(logits - top_policy[:, None])
    total = lax.optimization_barrier(jnp.sum(expo, axis=1))
    weighted = lax.optimization_barrier(jnp.sum(expo * (logits - refs), axis=1))
    top_ref = lax.optimization_barrier(jnp.max(refs, axis=1))
    ref_total = lax.optimization_barrier(jnp.sum(jnp.exp(refs - top_ref[:, None]), axis=1))
    lse_policy = top_policy + jnp.log(total)
    lse_ref = top_ref + jnp.log(ref_total)
    return weighted / total - lse_policy + lse_ref

def grad_rows(triple, head_weight):
    states, tokens, factor = triple
    logits = jnp.dot(states, head_weight, preferred_element_type=jnp.float32)
    top_policy = lax.optimization_barrier(jnp.max(logits, axis=1))
    lse_policy = top_policy + jnp.log(lax.optimization_barrier(jnp.sum(jnp.exp(logits - top_policy[:, None]), axis=1)))
    prob = jnp.exp(logits - lse_policy[:, None])
    column = jnp.arange(logits.shape[1]).astype(jnp.int32)
    onehot = (column[None, :] == tokens[:, None]).astype(jnp.float32)
    grad = (factor[:, None] * (prob - onehot)).astype(jnp.bfloat16)
    back = jnp.dot(grad, head_weight.T, preferred_element_type=jnp.float32).astype(jnp.bfloat16)
    return (grad, back)

def reference(hidden, head_weight, ref_logits, token_ids, end_pos, loss_mask, scores):
    kl_value = lax.map(lambda pair: row_stats(pair, head_weight), (hidden, ref_logits))
    position = jnp.arange(SEQ_LEN).astype(jnp.int32)
    live = ((loss_mask == 1) & (position[None, :] <= end_pos[:, None])).astype(jnp.float32)
    at_end = (position[None, :] == end_pos[:, None]).astype(jnp.float32)
    reward = -0.01 * kl_value * live + scores[:, None] * at_end
    returns = jnp.cumsum(reward[:, ::-1], axis=1)[:, ::-1]
    count = jnp.maximum(jnp.sum(live), 1.0)
    mean = jnp.sum(live * returns) / count
    var = jnp.sum(live * returns * returns) / count - mean * mean
    advantages = (returns - mean) / jnp.sqrt(var + 1e-05)
    factor = live * advantages / count
    logit_grad, hidden_grad = lax.map(lambda triple: grad_rows(triple, head_weight), (hidden, token_ids, factor))
    return (logit_grad, hidden_grad, advantages)
```

```python
import jax
import jax.numpy as jnp
from jax import lax
from jax.sharding import Mesh, PartitionSpec as P

SEQ = ("y", "c")
VOC = ("z", "x")
BOUNDS = ((0, 256), (256, 512), (512, 640))


def spread(value, axes):
    count = lax.axis_size(axes)
    return lax.all_to_all(jnp.broadcast_to(value[None], (count,) + value.shape), axes, 0, 0)


def per_device(hidden, head_weight, ref_logits, token_ids, end_pos, loss_mask, scores):
    batch, segment, width = hidden.shape
    rows = batch * segment
    depth, vocab_dev = head_weight.shape
    seqs = lax.axis_size(SEQ)
    seq_index = lax.axis_index(SEQ)
    seq_start = seq_index * segment
    vocab_start = lax.axis_index(VOC) * vocab_dev

    heads = [lax.all_gather(head_weight[lo:hi], SEQ, axis=0, tiled=True) for lo, hi in BOUNDS]

    refs = ref_logits.astype(jnp.float32).reshape(rows, vocab_dev)
    ref_top = jnp.max(refs, axis=1)
    ref_lse = ref_top + jnp.log(jnp.sum(jnp.exp(refs - ref_top[:, None]), axis=1))

    states = hidden.reshape(rows, seqs, depth)
    logits = None
    for (lo, hi), head in zip(BOUNDS, heads):
        term = jnp.dot(
            states[:, :, lo:hi].reshape(rows, seqs * (hi - lo)), head, preferred_element_type=jnp.float32
        )
        logits = term if logits is None else logits + term
    top = jnp.max(logits, axis=1)
    expo = jnp.exp(logits - top[:, None])
    stats = jnp.stack(
        [top, jnp.sum(expo, axis=1), jnp.sum(expo * (logits - refs), axis=1), ref_lse]
    )
    stats = spread(stats, VOC)
    tops = stats[:, 0]
    top_policy = jnp.max(tops, axis=0)
    scale = jnp.exp(tops - top_policy[None])
    total = jnp.sum(stats[:, 1] * scale, axis=0)
    weighted = jnp.sum(stats[:, 2] * scale, axis=0)
    top_ref = jnp.max(stats[:, 3], axis=0)
    lse_ref = top_ref + jnp.log(jnp.sum(jnp.exp(stats[:, 3] - top_ref[None]), axis=0))
    lse_policy = top_policy + jnp.log(total)
    kl_value = (weighted / total - lse_policy + lse_ref).reshape(batch, segment)

    position = seq_start + lax.broadcasted_iota(jnp.int32, (1, segment), 1)
    live = ((loss_mask == 1) & (position <= end_pos[:, None])).astype(jnp.float32)
    at_end = (position == end_pos[:, None]).astype(jnp.float32)
    reward = -0.01 * kl_value * live + scores[:, None] * at_end
    both = spread(jnp.stack([reward, live]), SEQ)
    rewards, lives = both[:, 0], both[:, 1]
    upper = (
        lax.broadcasted_iota(jnp.int32, (segment, segment), 0)
        >= lax.broadcasted_iota(jnp.int32, (segment, segment), 1)
    ).astype(jnp.float32)
    suffix = jnp.dot(
        rewards.reshape(seqs * batch, segment), upper, precision=lax.Precision.HIGHEST
    ).reshape(seqs, batch, segment)
    totals = jnp.sum(rewards, axis=2)
    later = (
        lax.broadcasted_iota(jnp.int32, (seqs, seqs, 1), 1)
        > lax.broadcasted_iota(jnp.int32, (seqs, seqs, 1), 0)
    ).astype(jnp.float32)
    carried = jnp.sum(later * totals[None], axis=1)
    returns_all = suffix + carried[:, :, None]
    count = jnp.maximum(jnp.sum(lives), 1.0)
    mean = jnp.sum(lives * returns_all) / count
    var = jnp.sum(lives * returns_all * returns_all) / count - mean * mean
    returns = lax.dynamic_index_in_dim(returns_all, seq_index, 0, keepdims=False)
    advantages = (returns - mean) / jnp.sqrt(var + 1e-05)
    factor = live * advantages / count

    prob = jnp.exp(logits - lse_policy[:, None])
    column = vocab_start + lax.broadcasted_iota(jnp.int32, (1, vocab_dev), 1)
    onehot = (column == token_ids.reshape(rows, 1)).astype(jnp.float32)
    logit_grad = (factor.reshape(rows, 1) * (prob - onehot)).astype(jnp.bfloat16)

    pieces = []
    for (lo, hi), head in zip(BOUNDS[::-1], heads[::-1]):
        part = lax.dot_general(
            head, logit_grad, (((1,), (1,)), ((), ())), preferred_element_type=jnp.float32
        ).reshape(seqs, hi - lo, rows)
        pieces.append(lax.psum_scatter(part, "z", scatter_dimension=0, tiled=False))
    mine = jnp.concatenate(pieces[::-1], axis=0)
    mine = mine.reshape(lax.axis_size("x"), depth // lax.axis_size("x"), rows)
    mine = lax.psum_scatter(mine, "x", scatter_dimension=0, tiled=False)
    hidden_grad = mine.T.reshape(batch, segment, -1).astype(jnp.bfloat16)
    return (logit_grad.reshape(batch, segment, vocab_dev), hidden_grad, advantages)


def solution(mesh):
    chips = mesh.devices.reshape(4, 2, 8, 4)
    fine = Mesh(chips, ("y", "c", "z", "x"))
    in_specs = (
        P(None, SEQ, None),
        P(SEQ, VOC),
        P(None, SEQ, VOC),
        P(None, SEQ),
        P(),
        P(None, SEQ),
        P(),
    )
    out_specs = (P(None, SEQ, VOC), P(None, SEQ, VOC), P(None, SEQ))
    return jax.shard_map(
        per_device, mesh=fine, in_specs=in_specs, out_specs=out_specs, check_vma=False
    )
```

```python
import functools

import jax
import jax.numpy as jnp
from jax import lax
from jax.experimental import pallas as pl
from jax.experimental.pallas import tpu as pltpu
from jax.sharding import Mesh, PartitionSpec as P

SEQ = ("y", "c")
VOC = ("z", "x")
STRIP = 16
TILE = 128


def spread(value, axes):
    count = lax.axis_size(axes)
    return lax.all_to_all(jnp.broadcast_to(value[None], (count,) + value.shape), axes, 0, 0)


def head_kernel(
    blocks, state_ref, ref_ref, token_ref, head_hbm, logit_ref, stat_ref, back_ref, head, expo, turned, sems
):
    rows, columns = logit_ref.shape
    depth = head.shape[0] // blocks
    parts = back_ref.shape[0]
    piece = depth // parts

    def fetch(block):
        span = pl.ds(pl.multiple_of(block * depth, depth), depth)
        return pltpu.make_async_copy(head_hbm.at[span], head.at[span], sems.at[block])

    for block in range(blocks):
        fetch(block).start()
    logit_ref[...] = jnp.zeros_like(logit_ref)

    @pl.loop(0, blocks)
    def _(block):
        fetch(block).wait()
        span = pl.ds(pl.multiple_of(block * depth, depth), depth)
        logit_ref[...] += jnp.dot(
            state_ref[:, span], head[span, :], preferred_element_type=jnp.float32
        )

    column = lax.broadcasted_iota(jnp.int32, (STRIP, columns), 1)
    lane = lax.broadcasted_iota(jnp.int32, (STRIP, TILE), 1)

    @pl.loop(0, rows // STRIP)
    def _(strip):
        span = pl.ds(pl.multiple_of(strip * STRIP, STRIP), STRIP)
        values = logit_ref[span, :]
        top = jnp.max(values, axis=1, keepdims=True)
        powers = jnp.exp(values - top)
        total = jnp.sum(powers, axis=1, keepdims=True)
        gap = values - ref_ref[span, :].astype(jnp.float32)
        weighted = jnp.sum(powers * gap, axis=1, keepdims=True)
        hit = column == token_ref[span, :]
        own = jnp.sum(jnp.where(hit, values, 0.0), axis=1, keepdims=True)
        expo[span, :] = jnp.where(hit, 0.0, powers)
        stat_ref[span, :] = jnp.where(
            lane == 0, top, jnp.where(lane == 1, total, jnp.where(lane == 2, weighted, own))
        )

    @pl.loop(0, columns // TILE)
    def _(tile):
        span = pl.ds(pl.multiple_of(tile * TILE, TILE), TILE)
        turned[span, :] = expo[:, span].T.astype(jnp.bfloat16)

    @pl.loop(0, blocks)
    def _(block):
        span = pl.ds(pl.multiple_of(block * depth, depth), depth)
        result = jnp.dot(head[span, :], turned[...], preferred_element_type=jnp.float32)
        result = result.astype(jnp.bfloat16)
        target = pl.ds(pl.multiple_of(block * piece, piece), piece)
        for part in range(parts):
            back_ref[part, target, :] = result[part * piece : (part + 1) * piece]


def run_head(states, refs, tokens, head, blocks, parts):
    rows, width = states.shape
    columns = head.shape[1]
    vmem = pl.BlockSpec(memory_space=pltpu.VMEM)
    return pl.pallas_call(
        functools.partial(head_kernel, blocks),
        out_shape=(
            jax.ShapeDtypeStruct((rows, columns), jnp.float32),
            jax.ShapeDtypeStruct((rows, TILE), jnp.float32),
            jax.ShapeDtypeStruct((parts, width // parts, rows), jnp.bfloat16),
        ),
        in_specs=[vmem, vmem, vmem, pl.BlockSpec(memory_space=pl.ANY)],
        out_specs=(vmem, vmem, vmem),
        scratch_shapes=[
            pltpu.VMEM((width, columns), jnp.bfloat16),
            pltpu.VMEM((rows, columns), jnp.float32),
            pltpu.VMEM((columns, rows), jnp.bfloat16),
            pltpu.SemaphoreType.DMA((blocks,)),
        ],
        compiler_params=pltpu.CompilerParams(vmem_limit_bytes=56 << 20),
        cost_estimate=pl.CostEstimate(
            flops=4 * rows * width * columns,
            bytes_accessed=2 * width * columns + 8 * rows * columns,
            transcendentals=rows * columns,
        ),
        name="head",
    )(states, refs, tokens, head)


def token_columns(head_weight, token_ids, vocab_start):
    depth, vocab_dev = head_weight.shape
    seqs, zs, xs = lax.axis_size(SEQ), lax.axis_size("z"), lax.axis_size("x")
    rows = token_ids.size
    ids = spread(token_ids.reshape(rows), SEQ).reshape(seqs * rows, 1)
    column = vocab_start + lax.broadcasted_iota(jnp.int32, (1, vocab_dev), 1)
    onehot = (column == ids).astype(jnp.bfloat16)
    found = lax.dot_general(
        head_weight, onehot, (((1,), (1,)), ((), ())), preferred_element_type=jnp.float32
    ).astype(jnp.bfloat16)
    found = found.reshape(xs, depth // xs, seqs, rows).transpose(0, 2, 1, 3)
    found = lax.all_to_all(found, "x", 0, 0)
    found = jnp.sum(found.astype(jnp.float32), axis=0).astype(jnp.bfloat16)
    found = lax.all_to_all(found, "z", 0, 0)
    found = jnp.sum(found.astype(jnp.float32), axis=0).astype(jnp.bfloat16)
    pairs = [(i * zs + j, j * zs + i) for i in range(seqs) for j in range(zs)]
    return lax.ppermute(found, SEQ + ("z",), pairs)


def per_device(hidden, head_weight, ref_logits, token_ids, end_pos, loss_mask, scores):
    batch, segment, width = hidden.shape
    rows = batch * segment
    vocab_dev = head_weight.shape[1]
    seqs, xs = lax.axis_size(SEQ), lax.axis_size("x")
    seq_index = lax.axis_index(SEQ)
    seq_start = seq_index * segment
    vocab_start = lax.axis_index(VOC) * vocab_dev

    whole_head = lax.all_gather(head_weight, SEQ, axis=0, tiled=True)
    own_columns = token_columns(head_weight, token_ids, vocab_start)

    refs = ref_logits.reshape(rows, vocab_dev)
    wide = refs.astype(jnp.float32)
    ref_top = jnp.max(wide, axis=1)
    ref_lse = ref_top + jnp.log(jnp.sum(jnp.exp(wide - ref_top[:, None]), axis=1))
    states, own_columns, ref_lse = lax.optimization_barrier(
        (hidden.reshape(rows, width), own_columns, ref_lse)
    )
    tokens = token_ids.reshape(rows, 1)
    logits, local, back = run_head(states, refs, tokens - vocab_start, whole_head, seqs, xs)

    stats = jnp.concatenate([local[:, :4].T, ref_lse[None]], axis=0)
    stats = spread(stats, VOC)
    back = lax.all_to_all(back, "x", 0, 0)

    tops = stats[:, 0]
    top_policy = jnp.max(tops, axis=0)
    scale = jnp.exp(tops - top_policy[None])
    total = jnp.sum(stats[:, 1] * scale, axis=0)
    weighted = jnp.sum(stats[:, 2] * scale, axis=0)
    own_logit = jnp.sum(stats[:, 3], axis=0)
    top_ref = jnp.max(stats[:, 4], axis=0)
    lse_ref = top_ref + jnp.log(jnp.sum(jnp.exp(stats[:, 4] - top_ref[None]), axis=0))
    lse_policy = top_policy + jnp.log(total)
    kl_value = (weighted / total - lse_policy + lse_ref).reshape(batch, segment)

    z_start = lax.axis_index("z") * xs
    share = lax.dynamic_slice_in_dim(scale, z_start, xs, 0) / total[None]
    back = back.reshape(xs, seqs, -1, rows)
    back = jnp.sum(back.astype(jnp.float32) * share[:, None, None, :], axis=0).astype(jnp.bfloat16)
    back = lax.all_to_all(back, "z", 0, 0)
    back = jnp.sum(back.astype(jnp.float32), axis=0)

    position = seq_start + lax.broadcasted_iota(jnp.int32, (1, segment), 1)
    live = ((loss_mask == 1) & (position <= end_pos[:, None])).astype(jnp.float32)
    at_end = (position == end_pos[:, None]).astype(jnp.float32)
    reward = -0.01 * kl_value * live + scores[:, None] * at_end
    both = spread(jnp.stack([reward, live]), SEQ)
    rewards, lives = both[:, 0], both[:, 1]
    upper = (
        lax.broadcasted_iota(jnp.int32, (segment, segment), 0)
        >= lax.broadcasted_iota(jnp.int32, (segment, segment), 1)
    ).astype(jnp.float32)
    suffix = jnp.dot(
        rewards.reshape(seqs * batch, segment), upper, precision=lax.Precision.HIGHEST
    ).reshape(seqs, batch, segment)
    totals = jnp.sum(rewards, axis=2)
    later = (
        lax.broadcasted_iota(jnp.int32, (seqs, seqs, 1), 1)
        > lax.broadcasted_iota(jnp.int32, (seqs, seqs, 1), 0)
    ).astype(jnp.float32)
    carried = jnp.sum(later * totals[None], axis=1)
    returns_all = suffix + carried[:, :, None]
    count = jnp.maximum(jnp.sum(lives), 1.0)
    mean = jnp.sum(lives * returns_all) / count
    var = jnp.sum(lives * returns_all * returns_all) / count - mean * mean
    returns = lax.dynamic_index_in_dim(returns_all, seq_index, 0, keepdims=False)
    advantages = (returns - mean) / jnp.sqrt(var + 1e-05)
    factor = (live * advantages / count).reshape(rows)

    prob = jnp.exp(logits - lse_policy[:, None])
    column = vocab_start + lax.broadcasted_iota(jnp.int32, (1, vocab_dev), 1)
    onehot = (column == tokens).astype(jnp.float32)
    logit_grad = (factor[:, None] * (prob - onehot)).astype(jnp.bfloat16)

    own_grad = (factor * (jnp.exp(own_logit - lse_policy) - 1.0)).astype(jnp.bfloat16)
    hidden_grad = factor[None] * back + own_grad.astype(jnp.float32)[None] * own_columns.astype(jnp.float32)
    hidden_grad = hidden_grad.T.reshape(batch, segment, -1).astype(jnp.bfloat16)
    return (logit_grad.reshape(batch, segment, vocab_dev), hidden_grad, advantages)


def solution(mesh):
    chips = mesh.devices.reshape(4, 2, 8, 4)
    fine = Mesh(chips, ("y", "c", "z", "x"))
    in_specs = (
        P(None, SEQ, None),
        P(SEQ, VOC),
        P(None, SEQ, VOC),
        P(None, SEQ),
        P(),
        P(None, SEQ),
        P(),
    )
    out_specs = (P(None, SEQ, VOC), P(None, SEQ, VOC), P(None, SEQ))
    return jax.shard_map(
        per_device, mesh=fine, in_specs=in_specs, out_specs=out_specs, check_vma=False
    )
```

```python
import functools

import jax
import jax.numpy as jnp
from jax import lax
from jax.experimental import pallas as pl
from jax.experimental.pallas import tpu as pltpu
from jax.sharding import Mesh, PartitionSpec as P

SEQ = ("y", "c")
VOC = ("z", "x")
TILE = 128
SUB = 8
WIDE = 8


def spread(value, axes):
    count = lax.axis_size(axes)
    return lax.all_to_all(jnp.broadcast_to(value[None], (count,) + value.shape), axes, 0, 0)


def head_kernel(blocks, place_ref, state_hbm, ref_hbm, token_ref, lse_ref, head_hbm,
                logit_hbm, stat_ref, back0, back1, back2, back3,
                state, refs, head, logit, flipped, turned, result, sems, outsem):
    rows, columns = logit.shape
    width = head.shape[0]
    depth = width // blocks
    backs = (back0, back1, back2, back3)
    parts = len(backs)
    piece = depth // parts
    wide = WIDE * TILE
    tiles = columns // wide
    tail = columns - tiles * wide

    def fetch(tile, size):
        span = pl.ds(pl.multiple_of(tile * wide, wide), size)
        return pltpu.make_async_copy(head_hbm.at[:, span], head.at[:, span], sems.at[tile])

    get_state = pltpu.make_async_copy(state_hbm, state, outsem.at[0])
    get_refs = pltpu.make_async_copy(ref_hbm, refs, outsem.at[1])
    get_state.start()
    for tile in range(tiles):
        fetch(tile, wide).start()
    if tail:
        fetch(tiles, tail).start()
    get_refs.start()
    get_state.wait()

    def forward(tile, size, best):
        fetch(tile, size).wait()
        span = pl.ds(pl.multiple_of(tile * wide, wide), size)
        values = jnp.dot(state[...], head[:, span], preferred_element_type=jnp.float32)
        logit[:, span] = values
        values = values.T
        flipped[span, :] = values
        return jnp.maximum(best, jnp.max(values.reshape(size // SUB, SUB, rows), axis=0))

    best = jnp.full((SUB, rows), -jnp.inf, jnp.float32)
    best = lax.fori_loop(0, tiles, lambda tile, best: forward(tile, wide, best), best)
    if tail:
        best = forward(tiles, tail, best)
    top = jnp.max(best, axis=0, keepdims=True)
    put_logit = pltpu.make_async_copy(logit, logit_hbm, outsem.at[0])
    put_logit.start()
    get_refs.wait()

    column = lax.broadcasted_iota(jnp.int32, (TILE, rows), 0)

    def fold(terms):
        return jnp.sum(terms.reshape(TILE // SUB, SUB, rows), axis=0)

    def strip(tile, sums):
        span = pl.ds(pl.multiple_of(tile * TILE, TILE), TILE)
        values = flipped[span, :]
        powers = jnp.exp(values - top)
        gap = values - refs[span, :].astype(jnp.float32)
        hit = column == token_ref[...] - tile * TILE
        turned[span, :] = jnp.where(hit, 0.0, powers).astype(jnp.bfloat16)
        return (
            sums[0] + fold(powers),
            sums[1] + fold(powers * gap),
            sums[2] + fold(jnp.where(hit, values, 0.0)),
        )

    zero = jnp.zeros((SUB, rows), jnp.float32)
    sums = lax.fori_loop(0, columns // TILE, strip, (zero, zero, zero))
    total, weighted, own = (jnp.sum(term, axis=0, keepdims=True) for term in sums)
    stats = jnp.concatenate([top, total, weighted, own, lse_ref[...], zero[:3]], axis=0)
    for device in range(stat_ref.shape[0]):
        stat_ref[device] = stats

    place = place_ref[0]

    @pl.loop(0, blocks)
    def _(block):
        span = pl.ds(pl.multiple_of(block * depth, depth), depth)
        result[...] = jnp.dot(
            head[span, :], turned[...], preferred_element_type=jnp.float32
        ).astype(jnp.bfloat16)
        target = pl.ds(pl.multiple_of(block * piece, piece), piece)
        for step, back in enumerate(backs):
            source = lax.rem(place + step, parts) * piece
            back[target, :] = result[pl.ds(pl.multiple_of(source, piece), piece), :]

    put_logit.wait()

def run_head(states, refs, tokens, ref_lse, place, head, blocks, parts, peers):
    rows, width = states.shape
    columns = head.shape[1]
    vmem = pl.BlockSpec(memory_space=pltpu.VMEM)
    hbm = pl.BlockSpec(memory_space=pl.ANY)
    back = jax.ShapeDtypeStruct((width // parts, rows), jnp.bfloat16)
    return pl.pallas_call(
        functools.partial(head_kernel, blocks),
        out_shape=(
            jax.ShapeDtypeStruct((rows, columns), jnp.float32),
            jax.ShapeDtypeStruct((peers, SUB, rows), jnp.float32),
        ) + (back,) * parts,
        in_specs=[pl.BlockSpec(memory_space=pltpu.SMEM), hbm, hbm, vmem, vmem, hbm],
        out_specs=(hbm,) + (vmem,) * (1 + parts),
        scratch_shapes=[
            pltpu.VMEM((rows, width), jnp.bfloat16),
            pltpu.VMEM((columns, rows), jnp.bfloat16),
            pltpu.VMEM((width, columns), jnp.bfloat16),
            pltpu.VMEM((rows, columns), jnp.float32),
            pltpu.VMEM((columns, rows), jnp.float32),
            pltpu.VMEM((columns, rows), jnp.bfloat16),
            pltpu.VMEM((width // blocks, rows), jnp.bfloat16),
            pltpu.SemaphoreType.DMA((-(-columns // (WIDE * TILE)),)),
            pltpu.SemaphoreType.DMA((2,)),
        ],
        compiler_params=pltpu.CompilerParams(vmem_limit_bytes=56 << 20),
        cost_estimate=pl.CostEstimate(
            flops=4 * rows * width * columns,
            bytes_accessed=2 * width * columns + 8 * rows * columns,
            transcendentals=rows * columns,
        ),
        name="head",
    )(place, states, refs, tokens, ref_lse, head)


def token_columns(head_weight, token_ids, vocab_start):
    depth, vocab_dev = head_weight.shape
    seqs, zs, xs = lax.axis_size(SEQ), lax.axis_size("z"), lax.axis_size("x")
    rows = token_ids.size
    ids = spread(token_ids.reshape(rows), SEQ).reshape(seqs * rows, 1)
    column = vocab_start + lax.broadcasted_iota(jnp.int32, (1, vocab_dev), 1)
    onehot = (column == ids).astype(jnp.bfloat16)
    found = lax.dot_general(
        head_weight, onehot, (((1,), (1,)), ((), ())), preferred_element_type=jnp.float32
    ).astype(jnp.bfloat16)
    found = found.reshape(xs, depth // xs, seqs, rows).transpose(0, 2, 1, 3)
    found = lax.all_to_all(found, "x", 0, 0)
    found = jnp.sum(found.astype(jnp.float32), axis=0).astype(jnp.bfloat16)
    found = lax.all_to_all(found, "z", 0, 0)
    found = jnp.sum(found.astype(jnp.float32), axis=0).astype(jnp.bfloat16)
    pairs = [(i * zs + j, j * zs + i) for i in range(seqs) for j in range(zs)]
    return lax.ppermute(found, SEQ + ("z",), pairs)


def per_device(hidden, head_weight, ref_logits, token_ids, end_pos, loss_mask, scores):
    batch, segment, width = hidden.shape
    rows = batch * segment
    vocab_dev = head_weight.shape[1]
    seqs, xs = lax.axis_size(SEQ), lax.axis_size("x")
    seq_index = lax.axis_index(SEQ)
    seq_start = seq_index * segment
    vocab_start = lax.axis_index(VOC) * vocab_dev

    whole_head = lax.all_gather(head_weight, SEQ, axis=0, tiled=True)
    own_columns = token_columns(head_weight, token_ids, vocab_start)

    refs = ref_logits.reshape(rows, vocab_dev)
    wide = refs.astype(jnp.float32)
    ref_top = jnp.max(wide, axis=1)
    ref_lse = ref_top + jnp.log(jnp.sum(jnp.exp(wide - ref_top[:, None]), axis=1))
    turned_refs = refs.T
    states, turned_refs, own_columns, ref_lse = lax.optimization_barrier(
        (hidden.reshape(rows, width), turned_refs, own_columns, ref_lse)
    )
    tokens = token_ids.reshape(rows, 1)
    x_index = lax.axis_index("x")
    logits, stats, *backs = run_head(
        states,
        turned_refs,
        (tokens - vocab_start).reshape(1, rows),
        ref_lse[None],
        x_index.reshape(1),
        whole_head,
        seqs,
        xs,
        lax.axis_size(VOC),
    )
    backs = [
        part if step == 0 else lax.ppermute(part, "x", [(i, (i + step) % xs) for i in range(xs)])
        for step, part in enumerate(backs)
    ]
    stats = lax.all_to_all(stats, VOC, 0, 0)

    tops = stats[:, 0]
    top_policy = jnp.max(tops, axis=0)
    scale = jnp.exp(tops - top_policy[None])
    total = jnp.sum(stats[:, 1] * scale, axis=0)
    weighted = jnp.sum(stats[:, 2] * scale, axis=0)
    own_logit = jnp.sum(stats[:, 3], axis=0)
    top_ref = jnp.max(stats[:, 4], axis=0)
    lse_ref = top_ref + jnp.log(jnp.sum(jnp.exp(stats[:, 4] - top_ref[None]), axis=0))
    lse_policy = top_policy + jnp.log(total)
    kl_value = (weighted / total - lse_policy + lse_ref).reshape(batch, segment)

    z_start = lax.axis_index("z") * xs
    back = 0.0
    for step, part in enumerate(backs):
        sender = z_start + lax.rem(x_index + xs - step, xs)
        share = lax.dynamic_index_in_dim(scale, sender, 0, keepdims=True) / total[None]
        back = back + part.astype(jnp.float32) * share
    back = back.astype(jnp.bfloat16).reshape(seqs, -1, rows)
    back = lax.all_to_all(back, "z", 0, 0)
    back = jnp.sum(back.astype(jnp.float32), axis=0)

    position = seq_start + lax.broadcasted_iota(jnp.int32, (1, segment), 1)
    live = ((loss_mask == 1) & (position <= end_pos[:, None])).astype(jnp.float32)
    at_end = (position == end_pos[:, None]).astype(jnp.float32)
    reward = -0.01 * kl_value * live + scores[:, None] * at_end
    both = spread(jnp.stack([reward, live]), SEQ)
    rewards, lives = both[:, 0], both[:, 1]
    upper = (
        lax.broadcasted_iota(jnp.int32, (segment, segment), 0)
        >= lax.broadcasted_iota(jnp.int32, (segment, segment), 1)
    ).astype(jnp.float32)
    suffix = jnp.dot(
        rewards.reshape(seqs * batch, segment), upper, precision=lax.Precision.HIGHEST
    ).reshape(seqs, batch, segment)
    totals = jnp.sum(rewards, axis=2)
    later = (
        lax.broadcasted_iota(jnp.int32, (seqs, seqs, 1), 1)
        > lax.broadcasted_iota(jnp.int32, (seqs, seqs, 1), 0)
    ).astype(jnp.float32)
    carried = jnp.sum(later * totals[None], axis=1)
    returns_all = suffix + carried[:, :, None]
    count = jnp.maximum(jnp.sum(lives), 1.0)
    mean = jnp.sum(lives * returns_all) / count
    var = jnp.sum(lives * returns_all * returns_all) / count - mean * mean
    returns = lax.dynamic_index_in_dim(returns_all, seq_index, 0, keepdims=False)
    advantages = (returns - mean) / jnp.sqrt(var + 1e-05)
    factor = (live * advantages / count).reshape(rows)

    prob = jnp.exp(logits - lse_policy[:, None])
    column = vocab_start + lax.broadcasted_iota(jnp.int32, (1, vocab_dev), 1)
    onehot = (column == tokens).astype(jnp.float32)
    logit_grad = (factor[:, None] * (prob - onehot)).astype(jnp.bfloat16)

    own_grad = (factor * (jnp.exp(own_logit - lse_policy) - 1.0)).astype(jnp.bfloat16)
    hidden_grad = factor[None] * back + own_grad.astype(jnp.float32)[None] * own_columns.astype(jnp.float32)
    hidden_grad = hidden_grad.T.reshape(batch, segment, -1).astype(jnp.bfloat16)
    return (logit_grad.reshape(batch, segment, vocab_dev), hidden_grad, advantages)


def solution(mesh):
    chips = mesh.devices.reshape(4, 2, 8, 4)
    fine = Mesh(chips, ("y", "c", "z", "x"))
    in_specs = (
        P(None, SEQ, None),
        P(SEQ, VOC),
        P(None, SEQ, VOC),
        P(None, SEQ),
        P(),
        P(None, SEQ),
        P(),
    )
    out_specs = (P(None, SEQ, VOC), P(None, SEQ, VOC), P(None, SEQ))
    return jax.shard_map(
        per_device, mesh=fine, in_specs=in_specs, out_specs=out_specs, check_vma=False
    )
```

```python
import functools

import jax
import jax.numpy as jnp
from jax import lax
from jax.experimental import pallas as pl
from jax.experimental.pallas import tpu as pltpu
from jax.sharding import Mesh, PartitionSpec as P

SEQ = ("y", "c")
VOC = ("z", "x")
TILE = 128
SUB = 8
WIDE = 8
FIRST = 48


def spread(value, axes):
    count = lax.axis_size(axes)
    return lax.all_to_all(jnp.broadcast_to(value[None], (count,) + value.shape), axes, 0, 0)


def rotate(value, axis, by):
    count = lax.axis_size(axis)
    return lax.ppermute(value, axis, [(i, (i + by) % count) for i in range(count)])


def head_kernel(blocks, pieces, first, place_ref, state_hbm, ref_hbm, token_ref, lse_ref, *rest):
    heads, rest = rest[:pieces], rest[pieces:]
    logit_hbm, stat_ref = rest[:2]
    parts = (len(rest) - 11) // 2
    early, late = rest[2 : 2 + parts], rest[2 + parts : 2 + 2 * parts]
    state, refs, head, logit, flipped, turned, result, sems, outsem = rest[2 + 2 * parts :]
    rows, columns = logit.shape
    width = head.shape[0]
    depth = width // blocks
    piece = depth // parts
    wide = WIDE * TILE
    tiles = columns // wide
    tail = columns - tiles * wide

    def fetch(tile, size):
        span = pl.ds(pl.multiple_of(tile * wide, wide), size)
        copies = []
        for index, part in enumerate(heads):
            start = pl.multiple_of(place_ref[1 + index], SUB * 4)
            place = pl.ds(start, part.shape[0])
            copies.append(
                pltpu.make_async_copy(part.at[:, span], head.at[place, span], sems.at[tile, index])
            )
        return copies

    get_state = pltpu.make_async_copy(state_hbm, state, outsem.at[0])
    get_refs = pltpu.make_async_copy(ref_hbm, refs, outsem.at[1])
    get_state.start()
    for tile in range(tiles):
        for copy in fetch(tile, wide):
            copy.start()
    if tail:
        for copy in fetch(tiles, tail):
            copy.start()
    get_refs.start()
    get_state.wait()

    def forward(tile, size, best):
        for copy in fetch(tile, size):
            copy.wait()
        span = pl.ds(pl.multiple_of(tile * wide, wide), size)
        values = jnp.dot(state[...], head[:, span], preferred_element_type=jnp.float32)
        logit[:, span] = values
        values = values.T
        flipped[span, :] = values
        return jnp.maximum(best, jnp.max(values.reshape(size // SUB, SUB, rows), axis=0))

    best = jnp.full((SUB, rows), -jnp.inf, jnp.float32)
    best = lax.fori_loop(0, tiles, lambda tile, best: forward(tile, wide, best), best)
    if tail:
        best = forward(tiles, tail, best)
    top = jnp.max(best, axis=0, keepdims=True)
    put_logit = pltpu.make_async_copy(logit, logit_hbm, outsem.at[0])
    put_logit.start()
    get_refs.wait()

    column = lax.broadcasted_iota(jnp.int32, (TILE, rows), 0)

    def fold(terms):
        return jnp.sum(terms.reshape(TILE // SUB, SUB, rows), axis=0)

    def strip(tile, sums):
        span = pl.ds(pl.multiple_of(tile * TILE, TILE), TILE)
        values = flipped[span, :]
        powers = jnp.exp(values - top)
        gap = values - refs[span, :].astype(jnp.float32)
        hit = column == token_ref[...] - tile * TILE
        turned[span, :] = jnp.where(hit, 0.0, powers).astype(jnp.bfloat16)
        return (
            sums[0] + fold(powers),
            sums[1] + fold(powers * gap),
            sums[2] + fold(jnp.where(hit, values, 0.0)),
        )

    zero = jnp.zeros((SUB, rows), jnp.float32)
    sums = lax.fori_loop(0, columns // TILE, strip, (zero, zero, zero))
    total, weighted, own = (jnp.sum(term, axis=0, keepdims=True) for term in sums)
    stats = jnp.concatenate([top, total, weighted, own, lse_ref[...], zero[:3]], axis=0)
    for device in range(stat_ref.shape[0]):
        stat_ref[device] = stats

    place = place_ref[0]

    @pl.loop(0, blocks)
    def _(block):
        span = pl.ds(pl.multiple_of(block * depth, depth), depth)
        result[...] = jnp.dot(
            head[span, :], turned[...], preferred_element_type=jnp.float32
        ).astype(jnp.bfloat16)
        for step in range(parts):
            source = lax.rem(place + step, parts) * piece
            for backs, offset, size in ((early, 0, first), (late, first, piece - first)):
                target = pl.ds(pl.multiple_of(block * size, SUB * 2), size)
                origin = pl.ds(pl.multiple_of(source + offset, SUB * 2), size)
                backs[step][target, :] = result[origin, :]

    put_logit.wait()

def run_head(states, refs, tokens, ref_lse, place, heads, blocks, parts, first, peers):
    rows, width = states.shape
    columns = heads[0].shape[1]
    vmem = pl.BlockSpec(memory_space=pltpu.VMEM)
    hbm = pl.BlockSpec(memory_space=pl.ANY)
    early = jax.ShapeDtypeStruct((blocks * first, rows), jnp.bfloat16)
    late = jax.ShapeDtypeStruct((width // parts - blocks * first, rows), jnp.bfloat16)
    return pl.pallas_call(
        functools.partial(head_kernel, blocks, len(heads), first),
        out_shape=(
            jax.ShapeDtypeStruct((rows, columns), jnp.float32),
            jax.ShapeDtypeStruct((peers, SUB, rows), jnp.float32),
        ) + (early,) * parts + (late,) * parts,
        in_specs=[pl.BlockSpec(memory_space=pltpu.SMEM), hbm, hbm, vmem, vmem] + [hbm] * len(heads),
        out_specs=(hbm,) + (vmem,) * (1 + 2 * parts),
        scratch_shapes=[
            pltpu.VMEM((rows, width), jnp.bfloat16),
            pltpu.VMEM((columns, rows), jnp.bfloat16),
            pltpu.VMEM((width, columns), jnp.bfloat16),
            pltpu.VMEM((rows, columns), jnp.float32),
            pltpu.VMEM((columns, rows), jnp.float32),
            pltpu.VMEM((columns, rows), jnp.bfloat16),
            pltpu.VMEM((width // blocks, rows), jnp.bfloat16),
            pltpu.SemaphoreType.DMA((-(-columns // (WIDE * TILE)), len(heads))),
            pltpu.SemaphoreType.DMA((2,)),
        ],
        compiler_params=pltpu.CompilerParams(vmem_limit_bytes=56 << 20),
        cost_estimate=pl.CostEstimate(
            flops=4 * rows * width * columns,
            bytes_accessed=2 * width * columns + 8 * rows * columns,
            transcendentals=rows * columns,
        ),
        name="head",
    )(place, states, refs, tokens, ref_lse, *heads)


def merge(stats):
    top = jnp.max(stats[:, 0], axis=0)
    scale = jnp.exp(stats[:, 0] - top[None])
    total = jnp.sum(stats[:, 1] * scale, axis=0)
    weighted = jnp.sum(stats[:, 2] * scale, axis=0)
    own = jnp.sum(stats[:, 3], axis=0)
    ref_top = jnp.max(stats[:, 4], axis=0)
    ref_lse = ref_top + jnp.log(jnp.sum(jnp.exp(stats[:, 4] - ref_top[None]), axis=0))
    return top, total, weighted, own, ref_lse


def gather_head(head_weight):
    depth = head_weight.shape[0]
    half = depth // 2
    ys, cores = lax.axis_size("y"), lax.axis_size("c")
    y, core = lax.axis_index("y"), lax.axis_index("c")
    upper, lower = head_weight[:half], head_weight[half:]
    near = [rotate(upper, "y", 1), rotate(lower, "y", -1)]
    late = [rotate(lower, "y", 1), rotate(upper, "y", -1)]
    far = [rotate(near[0], "y", 1), rotate(near[1], "y", -1)]
    found = [(head_weight, 0, 0)]
    found += [(near[0], -1, 0), (near[1], 1, half), (late[0], -1, half), (late[1], 1, 0)]
    found += [(far[0], -2, 0), (far[1], 2, half)]
    pieces, starts = [], []
    for piece, step, row in found:
        chip = lax.rem(y + step + ys, ys)
        for other in (0, 1):
            owner = chip * cores + (core if other == 0 else 1 - core)
            pieces.append(piece if other == 0 else rotate(piece, "c", 1))
            starts.append(owner * depth + row)
    return pieces, starts, near


def token_columns(head_weight, token_ids, vocab_start, near):
    depth, vocab_dev = head_weight.shape
    seqs, zs, xs = lax.axis_size(SEQ), lax.axis_size("z"), lax.axis_size("x")
    rows = token_ids.size
    ids = spread(token_ids.reshape(rows), SEQ).reshape(seqs * rows, 1)
    column = vocab_start + lax.broadcasted_iota(jnp.int32, (1, vocab_dev), 1)
    onehot = (column == ids).astype(jnp.bfloat16)
    found = lax.dot_general(
        head_weight, onehot, (((1,), (1,)), ((), ())), preferred_element_type=jnp.float32
    ).astype(jnp.bfloat16)
    found = found.reshape(xs, depth // xs, seqs, rows).transpose(0, 2, 1, 3)
    found, near = lax.optimization_barrier((found, near))
    found = lax.all_to_all(found, "x", 0, 0)
    found = jnp.sum(found.astype(jnp.float32), axis=0).astype(jnp.bfloat16)
    found = lax.all_to_all(found, "z", 0, 0)
    found = jnp.sum(found.astype(jnp.float32), axis=0).astype(jnp.bfloat16)
    pairs = [(i * zs + j, j * zs + i) for i in range(seqs) for j in range(zs)]
    return lax.ppermute(found, SEQ + ("z",), pairs)


def per_device(hidden, head_weight, ref_logits, token_ids, end_pos, loss_mask, scores):
    batch, segment, width = hidden.shape
    rows = batch * segment
    vocab_dev = head_weight.shape[1]
    seqs, xs = lax.axis_size(SEQ), lax.axis_size("x")
    seq_index = lax.axis_index(SEQ)
    seq_start = seq_index * segment
    vocab_start = lax.axis_index(VOC) * vocab_dev

    heads, starts, near = gather_head(head_weight)
    own_columns = token_columns(head_weight, token_ids, vocab_start, near)

    refs = ref_logits.reshape(rows, vocab_dev)
    wide = refs.astype(jnp.float32)
    ref_top = jnp.max(wide, axis=1)
    ref_lse = ref_top + jnp.log(jnp.sum(jnp.exp(wide - ref_top[:, None]), axis=1))
    turned_refs = refs.T
    states, turned_refs, own_columns, ref_lse = lax.optimization_barrier(
        (hidden.reshape(rows, width), turned_refs, own_columns, ref_lse)
    )
    tokens = token_ids.reshape(rows, 1)
    x_index = lax.axis_index("x")
    logits, stats, *backs = run_head(
        states,
        turned_refs,
        (tokens - vocab_start).reshape(1, rows),
        ref_lse[None],
        jnp.stack([x_index] + starts),
        heads,
        seqs,
        xs,
        FIRST,
        xs,
    )
    early, late = (
        [part if step == 0 else rotate(part, "x", step) for step, part in enumerate(group)]
        for group in (backs[:xs], backs[xs:])
    )
    stats = lax.all_to_all(stats, "x", 0, 0)
    tops = stats[:, 0]
    merged, early = lax.optimization_barrier((jnp.stack(merge(stats)), early))
    stats = spread(merged, "z")
    top_policy, total, weighted, own_logit, lse_ref = merge(stats)
    lse_policy = top_policy + jnp.log(total)
    kl_value = (weighted / total - lse_policy + lse_ref).reshape(batch, segment)

    share = jnp.exp(tops - top_policy[None]) / total[None]
    gathered = []
    for group in (early, late):
        back = 0.0
        for step, part in enumerate(group):
            sender = lax.rem(x_index + xs - step, xs)
            back = back + part.astype(jnp.float32) * lax.dynamic_slice_in_dim(share, sender, 1, 0)
        back = back.astype(jnp.bfloat16).reshape(seqs, -1, rows)
        back = lax.all_to_all(back, "z", 0, 0)
        gathered.append(jnp.sum(back.astype(jnp.float32), axis=0))
    back = jnp.concatenate(gathered, axis=0)

    position = seq_start + lax.broadcasted_iota(jnp.int32, (1, segment), 1)
    live = ((loss_mask == 1) & (position <= end_pos[:, None])).astype(jnp.float32)
    at_end = (position == end_pos[:, None]).astype(jnp.float32)
    reward = -0.01 * kl_value * live + scores[:, None] * at_end
    both = spread(jnp.stack([reward, live]), SEQ)
    rewards, lives = both[:, 0], both[:, 1]
    upper = (
        lax.broadcasted_iota(jnp.int32, (segment, segment), 0)
        >= lax.broadcasted_iota(jnp.int32, (segment, segment), 1)
    ).astype(jnp.float32)
    suffix = jnp.dot(
        rewards.reshape(seqs * batch, segment), upper, precision=lax.Precision.HIGHEST
    ).reshape(seqs, batch, segment)
    totals = jnp.sum(rewards, axis=2)
    later = (
        lax.broadcasted_iota(jnp.int32, (seqs, seqs, 1), 1)
        > lax.broadcasted_iota(jnp.int32, (seqs, seqs, 1), 0)
    ).astype(jnp.float32)
    carried = jnp.sum(later * totals[None], axis=1)
    returns_all = suffix + carried[:, :, None]
    count = jnp.maximum(jnp.sum(lives), 1.0)
    mean = jnp.sum(lives * returns_all) / count
    var = jnp.sum(lives * returns_all * returns_all) / count - mean * mean
    returns = lax.dynamic_index_in_dim(returns_all, seq_index, 0, keepdims=False)
    advantages = (returns - mean) / jnp.sqrt(var + 1e-05)
    factor = (live * advantages / count).reshape(rows)

    prob = jnp.exp(logits - lse_policy[:, None])
    column = vocab_start + lax.broadcasted_iota(jnp.int32, (1, vocab_dev), 1)
    onehot = (column == tokens).astype(jnp.float32)
    logit_grad = (factor[:, None] * (prob - onehot)).astype(jnp.bfloat16)

    own_grad = (factor * (jnp.exp(own_logit - lse_policy) - 1.0)).astype(jnp.bfloat16)
    hidden_grad = factor[None] * back + own_grad.astype(jnp.float32)[None] * own_columns.astype(jnp.float32)
    hidden_grad = hidden_grad.T.reshape(batch, segment, -1).astype(jnp.bfloat16)
    return (logit_grad.reshape(batch, segment, vocab_dev), hidden_grad, advantages)


def solution(mesh):
    chips = mesh.devices.reshape(4, 2, 8, 4)
    fine = Mesh(chips, ("y", "c", "z", "x"))
    in_specs = (
        P(None, SEQ, None),
        P(SEQ, VOC),
        P(None, SEQ, VOC),
        P(None, SEQ),
        P(),
        P(None, SEQ),
        P(),
    )
    out_specs = (P(None, SEQ, VOC), P(None, SEQ, VOC), P(None, SEQ))
    return jax.shard_map(
        per_device, mesh=fine, in_specs=in_specs, out_specs=out_specs, check_vma=False
    )
```

```python
import functools

import jax
import jax.numpy as jnp
from jax import lax
from jax.experimental import pallas as pl
from jax.experimental.pallas import tpu as pltpu
from jax.sharding import Mesh, PartitionSpec as P

SEQ = ("y", "c")
VOC = ("z", "x")
TILE = 128
SUB = 8
WIDE = 8
FIRST = 112


def spread(value, axes):
    count = lax.axis_size(axes)
    return lax.all_to_all(jnp.broadcast_to(value[None], (count,) + value.shape), axes, 0, 0)


def share_out(value, axes):
    slots = lax.broadcasted_iota(jnp.int32, (lax.axis_size(axes),) + (1,) * value.ndim, 0)
    return lax.psum(jnp.where(slots == lax.axis_index(axes), value[None], 0.0), axes)


def rotate(value, axis, by):
    count = lax.axis_size(axis)
    return lax.ppermute(value, axis, [(i, (i + by) % count) for i in range(count)])


def head_kernel(blocks, place_ref, state_hbm, ref_hbm, token_ref, lse_ref, head_hbm,
                logit_hbm, stat_ref, back0, back1, back2, back3, by_block,
                state, refs, head, logit, flipped, turned, result, sems, outsem):
    rows, columns = logit.shape
    width = head.shape[0]
    depth = width // blocks
    backs = (back0, back1, back2, back3)
    parts = len(backs)
    piece = depth // parts
    first = back0.shape[0] // blocks
    wide = WIDE * TILE
    tiles = columns // wide
    tail = columns - tiles * wide

    def fetch(tile, size):
        span = pl.ds(pl.multiple_of(tile * wide, wide), size)
        return pltpu.make_async_copy(head_hbm.at[:, span], head.at[:, span], sems.at[tile])

    get_state = pltpu.make_async_copy(state_hbm, state, outsem.at[0])
    get_refs = pltpu.make_async_copy(ref_hbm, refs, outsem.at[1])
    get_state.start()
    for tile in range(tiles):
        fetch(tile, wide).start()
    if tail:
        fetch(tiles, tail).start()
    get_refs.start()
    get_state.wait()

    def forward(tile, size, best):
        fetch(tile, size).wait()
        span = pl.ds(pl.multiple_of(tile * wide, wide), size)
        values = jnp.dot(state[...], head[:, span], preferred_element_type=jnp.float32)
        logit[:, span] = values
        values = values.T
        flipped[span, :] = values
        return jnp.maximum(best, jnp.max(values.reshape(size // SUB, SUB, rows), axis=0))

    best = jnp.full((SUB, rows), -jnp.inf, jnp.float32)
    best = lax.fori_loop(0, tiles, lambda tile, best: forward(tile, wide, best), best)
    if tail:
        best = forward(tiles, tail, best)
    top = jnp.max(best, axis=0, keepdims=True)
    put_logit = pltpu.make_async_copy(logit, logit_hbm, outsem.at[0])
    put_logit.start()
    get_refs.wait()

    column = lax.broadcasted_iota(jnp.int32, (TILE, rows), 0)

    def fold(terms):
        return jnp.sum(terms.reshape(TILE // SUB, SUB, rows), axis=0)

    def strip(tile, sums):
        span = pl.ds(pl.multiple_of(tile * TILE, TILE), TILE)
        values = flipped[span, :]
        powers = jnp.exp(values - top)
        gap = values - refs[span, :].astype(jnp.float32)
        hit = column == token_ref[...] - tile * TILE
        turned[span, :] = jnp.where(hit, 0.0, powers).astype(jnp.bfloat16)
        return (
            sums[0] + fold(powers),
            sums[1] + fold(powers * gap),
            sums[2] + fold(jnp.where(hit, values, 0.0)),
        )

    zero = jnp.zeros((SUB, rows), jnp.float32)
    sums = lax.fori_loop(0, columns // TILE, strip, (zero, zero, zero))
    total, weighted, own = (jnp.sum(term, axis=0, keepdims=True) for term in sums)
    stats = jnp.concatenate([top, total, weighted, own, lse_ref[...], zero[:3]], axis=0)
    for device in range(stat_ref.shape[0]):
        stat_ref[device] = stats

    place = place_ref[0]

    @pl.loop(0, blocks)
    def _(block):
        span = pl.ds(pl.multiple_of(block * depth, depth), depth)
        result[...] = jnp.dot(
            head[span, :], turned[...], preferred_element_type=jnp.float32
        ).astype(jnp.bfloat16)
        target = pl.ds(pl.multiple_of(block * first, SUB * 2), first)
        for part, back in enumerate(backs):
            source = lax.rem(place + part, parts) * piece
            back[target, :] = result[pl.ds(pl.multiple_of(source, SUB * 4), first), :]
            by_block[block, part * (piece - first) : (part + 1) * (piece - first), :] = result[
                part * piece + first : (part + 1) * piece, :
            ]

    put_logit.wait()

def run_head(states, refs, tokens, ref_lse, place, head, blocks, parts, first, peers):
    rows, width = states.shape
    columns = head.shape[1]
    vmem = pl.BlockSpec(memory_space=pltpu.VMEM)
    hbm = pl.BlockSpec(memory_space=pl.ANY)
    back = jax.ShapeDtypeStruct((blocks * first, rows), jnp.bfloat16)
    rest = width // blocks - parts * first
    return pl.pallas_call(
        functools.partial(head_kernel, blocks),
        out_shape=(
            jax.ShapeDtypeStruct((rows, columns), jnp.float32),
            jax.ShapeDtypeStruct((peers, SUB, rows), jnp.float32),
        ) + (back,) * parts + (jax.ShapeDtypeStruct((blocks, rest, rows), jnp.bfloat16),),
        in_specs=[pl.BlockSpec(memory_space=pltpu.SMEM), hbm, hbm, vmem, vmem, hbm],
        out_specs=(hbm,) + (vmem,) * (2 + parts),
        scratch_shapes=[
            pltpu.VMEM((rows, width), jnp.bfloat16),
            pltpu.VMEM((columns, rows), jnp.bfloat16),
            pltpu.VMEM((width, columns), jnp.bfloat16),
            pltpu.VMEM((rows, columns), jnp.float32),
            pltpu.VMEM((columns, rows), jnp.float32),
            pltpu.VMEM((columns, rows), jnp.bfloat16),
            pltpu.VMEM((width // blocks, rows), jnp.bfloat16),
            pltpu.SemaphoreType.DMA((-(-columns // (WIDE * TILE)),)),
            pltpu.SemaphoreType.DMA((2,)),
        ],
        compiler_params=pltpu.CompilerParams(vmem_limit_bytes=56 << 20),
        cost_estimate=pl.CostEstimate(
            flops=4 * rows * width * columns,
            bytes_accessed=2 * width * columns + 8 * rows * columns,
            transcendentals=rows * columns,
        ),
        name="head",
    )(place, states, refs, tokens, ref_lse, head)


def token_columns(head_weight, token_ids, vocab_start):
    depth, vocab_dev = head_weight.shape
    seqs, zs, xs = lax.axis_size(SEQ), lax.axis_size("z"), lax.axis_size("x")
    rows = token_ids.size
    ids = spread(token_ids.reshape(rows), SEQ).reshape(seqs * rows, 1)
    column = vocab_start + lax.broadcasted_iota(jnp.int32, (1, vocab_dev), 1)
    onehot = (column == ids).astype(jnp.bfloat16)
    found = lax.dot_general(
        head_weight, onehot, (((1,), (1,)), ((), ())), preferred_element_type=jnp.float32
    ).astype(jnp.bfloat16)
    found = found.reshape(xs, depth // xs, seqs, rows).transpose(0, 2, 1, 3)
    found = lax.all_to_all(found, "x", 0, 0)
    found = jnp.sum(found.astype(jnp.float32), axis=0).astype(jnp.bfloat16)
    found = lax.all_to_all(found, "z", 0, 0)
    found = jnp.sum(found.astype(jnp.float32), axis=0).astype(jnp.bfloat16)
    pairs = [(i * zs + j, j * zs + i) for i in range(seqs) for j in range(zs)]
    return lax.ppermute(found, SEQ + ("z",), pairs)


def per_device(hidden, head_weight, ref_logits, token_ids, end_pos, loss_mask, scores):
    batch, segment, width = hidden.shape
    rows = batch * segment
    vocab_dev = head_weight.shape[1]
    seqs, xs = lax.axis_size(SEQ), lax.axis_size("x")
    seq_index = lax.axis_index(SEQ)
    seq_start = seq_index * segment
    vocab_start = lax.axis_index(VOC) * vocab_dev

    whole_head = lax.all_gather(head_weight, SEQ, axis=0, tiled=True)
    own_columns = token_columns(head_weight, token_ids, vocab_start)

    refs = ref_logits.reshape(rows, vocab_dev)
    wide = refs.astype(jnp.float32)
    ref_top = jnp.max(wide, axis=1)
    ref_lse = ref_top + jnp.log(jnp.sum(jnp.exp(wide - ref_top[:, None]), axis=1))
    turned_refs = refs.T
    states, turned_refs, own_columns, ref_lse = lax.optimization_barrier(
        (hidden.reshape(rows, width), turned_refs, own_columns, ref_lse)
    )
    tokens = token_ids.reshape(rows, 1)
    x_index = lax.axis_index("x")
    logits, stats, *backs, other = run_head(
        states,
        turned_refs,
        (tokens - vocab_start).reshape(1, rows),
        ref_lse[None],
        x_index.reshape(1),
        whole_head,
        seqs,
        xs,
        FIRST,
        lax.axis_size(VOC),
    )
    backs = [part if step == 0 else rotate(part, "x", step) for step, part in enumerate(backs)]
    stats = lax.all_to_all(stats, VOC, 0, 0)
    stats, other = lax.optimization_barrier((stats, other))
    other = lax.all_to_all(other, "z", 0, 0)

    tops = stats[:, 0]
    top_policy = jnp.max(tops, axis=0)
    scale = jnp.exp(tops - top_policy[None])
    total = jnp.sum(stats[:, 1] * scale, axis=0)
    weighted = jnp.sum(stats[:, 2] * scale, axis=0)
    own_logit = jnp.sum(stats[:, 3], axis=0)
    top_ref = jnp.max(stats[:, 4], axis=0)
    lse_ref = top_ref + jnp.log(jnp.sum(jnp.exp(stats[:, 4] - top_ref[None]), axis=0))
    lse_policy = top_policy + jnp.log(total)
    kl_value = (weighted / total - lse_policy + lse_ref).reshape(batch, segment)

    zs, z_index = lax.axis_size("z"), lax.axis_index("z")
    share = (scale / total[None]).reshape(zs, xs, rows)
    here = lax.dynamic_index_in_dim(share, z_index, 0, keepdims=False)
    back = 0.0
    for step, part in enumerate(backs):
        sender = lax.rem(x_index + xs - step, xs)
        back = back + part.astype(jnp.float32) * lax.dynamic_slice_in_dim(here, sender, 1, 0)
    back = back.astype(jnp.bfloat16).reshape(zs, -1, rows)
    back = lax.all_to_all(back, "z", 0, 0)
    back = jnp.sum(back.astype(jnp.float32), axis=0)

    here = lax.dynamic_index_in_dim(share, x_index, 1, keepdims=True)
    other = jnp.sum(other.astype(jnp.float32) * here, axis=0).astype(jnp.bfloat16)
    other = other.reshape(xs, -1, rows)
    mine = 0.0
    for step in range(xs):
        part = lax.dynamic_index_in_dim(other, lax.rem(x_index + step, xs), 0, keepdims=False)
        mine = mine + (part if step == 0 else rotate(part, "x", step)).astype(jnp.float32)
    back = jnp.concatenate([back, mine], axis=0)

    position = seq_start + lax.broadcasted_iota(jnp.int32, (1, segment), 1)
    live = ((loss_mask == 1) & (position <= end_pos[:, None])).astype(jnp.float32)
    at_end = (position == end_pos[:, None]).astype(jnp.float32)
    reward = -0.01 * kl_value * live + scores[:, None] * at_end
    both = share_out(jnp.stack([reward, live]), SEQ)
    rewards, lives = both[:, 0], both[:, 1]
    upper = (
        lax.broadcasted_iota(jnp.int32, (segment, segment), 0)
        >= lax.broadcasted_iota(jnp.int32, (segment, segment), 1)
    ).astype(jnp.float32)
    suffix = jnp.dot(
        rewards.reshape(seqs * batch, segment), upper, precision=lax.Precision.HIGHEST
    ).reshape(seqs, batch, segment)
    totals = jnp.sum(rewards, axis=2)
    later = (
        lax.broadcasted_iota(jnp.int32, (seqs, seqs, 1), 1)
        > lax.broadcasted_iota(jnp.int32, (seqs, seqs, 1), 0)
    ).astype(jnp.float32)
    carried = jnp.sum(later * totals[None], axis=1)
    returns_all = suffix + carried[:, :, None]
    count = jnp.maximum(jnp.sum(lives), 1.0)
    mean = jnp.sum(lives * returns_all) / count
    var = jnp.sum(lives * returns_all * returns_all) / count - mean * mean
    returns = lax.dynamic_index_in_dim(returns_all, seq_index, 0, keepdims=False)
    advantages = (returns - mean) / jnp.sqrt(var + 1e-05)
    factor = (live * advantages / count).reshape(rows)

    prob = jnp.exp(logits - lse_policy[:, None])
    column = vocab_start + lax.broadcasted_iota(jnp.int32, (1, vocab_dev), 1)
    onehot = (column == tokens).astype(jnp.float32)
    logit_grad = (factor[:, None] * (prob - onehot)).astype(jnp.bfloat16)

    own_grad = (factor * (jnp.exp(own_logit - lse_policy) - 1.0)).astype(jnp.bfloat16)
    hidden_grad = factor[None] * back + own_grad.astype(jnp.float32)[None] * own_columns.astype(jnp.float32)
    hidden_grad = hidden_grad.T.reshape(batch, segment, -1).astype(jnp.bfloat16)
    return (logit_grad.reshape(batch, segment, vocab_dev), hidden_grad, advantages)


def solution(mesh):
    chips = mesh.devices.reshape(4, 2, 8, 4)
    fine = Mesh(chips, ("y", "c", "z", "x"))
    in_specs = (
        P(None, SEQ, None),
        P(SEQ, VOC),
        P(None, SEQ, VOC),
        P(None, SEQ),
        P(),
        P(None, SEQ),
        P(),
    )
    out_specs = (P(None, SEQ, VOC), P(None, SEQ, VOC), P(None, SEQ))
    return jax.shard_map(
        per_device, mesh=fine, in_specs=in_specs, out_specs=out_specs, check_vma=False
    )
```

```python
import functools

import jax
import jax.numpy as jnp
from jax import lax
from jax.experimental import pallas as pl
from jax.experimental.pallas import tpu as pltpu
from jax.sharding import Mesh, PartitionSpec as P

SEQ = ("y", "c")
VOC = ("z", "x")
TILE = 128
SUB = 8
FIRST = 112


def spread(value, axes):
    count = lax.axis_size(axes)
    return lax.all_to_all(jnp.broadcast_to(value[None], (count,) + value.shape), axes, 0, 0)


def rotate(value, axis, by):
    count = lax.axis_size(axis)
    return lax.ppermute(value, axis, [(i, (i + by) % count) for i in range(count)])


def head_kernel(sizes, place_ref, state_hbm, ref_hbm, token_ref, lse_ref, *rest):
    count, blocks = sum(sizes), len(sizes)
    heads, rest = rest[:count], rest[count:]
    logit_hbm, stat_ref, back0, back1, back2, back3, by_block = rest[:7]
    state, refs, head, logit, flipped, turned, result, sems, outsem = rest[7:]
    rows, columns = logit.shape
    width = head.shape[0]
    depth = width // blocks
    backs = (back0, back1, back2, back3)
    parts = len(backs)
    piece = depth // parts
    first = back0.shape[0] // blocks

    get_state = pltpu.make_async_copy(state_hbm, state, outsem.at[0])
    get_refs = pltpu.make_async_copy(ref_hbm, refs, outsem.at[1])
    get_state.start()
    fetches, at = [], 0
    for block, size in enumerate(sizes):
        start = pl.multiple_of(place_ref[1 + block] * depth, depth)
        copies = []
        for part in heads[at : at + size]:
            span = pl.ds(start, part.shape[0])
            copies.append(pltpu.make_async_copy(part, head.at[span], sems.at[at]))
            copies[-1].start()
            start = pl.multiple_of(start + part.shape[0], SUB * 4)
            at += 1
        fetches.append(copies)
    get_refs.start()
    get_state.wait()

    for block, copies in enumerate(fetches):
        for copy in copies:
            copy.wait()
        span = pl.ds(pl.multiple_of(place_ref[1 + block] * depth, depth), depth)
        term = jnp.dot(state[:, span], head[span, :], preferred_element_type=jnp.float32)
        logit[...] = term if block == 0 else logit[...] + term
    put_logit = pltpu.make_async_copy(logit, logit_hbm, outsem.at[0])
    put_logit.start()

    def flip(tile, best):
        span = pl.ds(pl.multiple_of(tile * TILE, TILE), TILE)
        values = logit[:, span].T
        flipped[span, :] = values
        return jnp.maximum(best, jnp.max(values.reshape(TILE // SUB, SUB, rows), axis=0))

    best = jnp.full((SUB, rows), -jnp.inf, jnp.float32)
    best = lax.fori_loop(0, columns // TILE, flip, best)
    top = jnp.max(best, axis=0, keepdims=True)
    get_refs.wait()

    column = lax.broadcasted_iota(jnp.int32, (TILE, rows), 0)

    def fold(terms):
        return jnp.sum(terms.reshape(TILE // SUB, SUB, rows), axis=0)

    def strip(tile, sums):
        span = pl.ds(pl.multiple_of(tile * TILE, TILE), TILE)
        values = flipped[span, :]
        powers = jnp.exp(values - top)
        gap = values - refs[span, :].astype(jnp.float32)
        hit = column == token_ref[...] - tile * TILE
        turned[span, :] = jnp.where(hit, 0.0, powers).astype(jnp.bfloat16)
        return (
            sums[0] + fold(powers),
            sums[1] + fold(powers * gap),
            sums[2] + fold(jnp.where(hit, values, 0.0)),
        )

    zero = jnp.zeros((SUB, rows), jnp.float32)
    sums = lax.fori_loop(0, columns // TILE, strip, (zero, zero, zero))
    total, weighted, own = (jnp.sum(term, axis=0, keepdims=True) for term in sums)
    stats = jnp.concatenate([top, total, weighted, own, lse_ref[...], zero[:3]], axis=0)
    for device in range(stat_ref.shape[0]):
        stat_ref[device] = stats

    place = place_ref[0]

    @pl.loop(0, blocks)
    def _(block):
        span = pl.ds(pl.multiple_of(block * depth, depth), depth)
        result[...] = jnp.dot(
            head[span, :], turned[...], preferred_element_type=jnp.float32
        ).astype(jnp.bfloat16)
        target = pl.ds(pl.multiple_of(block * first, SUB * 2), first)
        for part, back in enumerate(backs):
            source = lax.rem(place + part, parts) * piece
            back[target, :] = result[pl.ds(pl.multiple_of(source, SUB * 4), first), :]
            by_block[block, part * (piece - first) : (part + 1) * (piece - first), :] = result[
                part * piece + first : (part + 1) * piece, :
            ]

    put_logit.wait()

def run_head(states, refs, tokens, ref_lse, place, shards, parts, first, peers):
    heads = [part for shard in shards for part in shard]
    blocks = len(shards)
    rows, width = states.shape
    columns = heads[0].shape[1]
    vmem = pl.BlockSpec(memory_space=pltpu.VMEM)
    hbm = pl.BlockSpec(memory_space=pl.ANY)
    back = jax.ShapeDtypeStruct((blocks * first, rows), jnp.bfloat16)
    rest = width // blocks - parts * first
    return pl.pallas_call(
        functools.partial(head_kernel, tuple(len(shard) for shard in shards)),
        out_shape=(
            jax.ShapeDtypeStruct((rows, columns), jnp.float32),
            jax.ShapeDtypeStruct((peers, SUB, rows), jnp.float32),
        ) + (back,) * parts + (jax.ShapeDtypeStruct((blocks, rest, rows), jnp.bfloat16),),
        in_specs=[pl.BlockSpec(memory_space=pltpu.SMEM), hbm, hbm, vmem, vmem] + [hbm] * len(heads),
        out_specs=(hbm,) + (vmem,) * (2 + parts),
        scratch_shapes=[
            pltpu.VMEM((rows, width), jnp.bfloat16),
            pltpu.VMEM((columns, rows), jnp.bfloat16),
            pltpu.VMEM((width, columns), jnp.bfloat16),
            pltpu.VMEM((rows, columns), jnp.float32),
            pltpu.VMEM((columns, rows), jnp.float32),
            pltpu.VMEM((columns, rows), jnp.bfloat16),
            pltpu.VMEM((width // blocks, rows), jnp.bfloat16),
            pltpu.SemaphoreType.DMA((len(heads),)),
            pltpu.SemaphoreType.DMA((2,)),
        ],
        compiler_params=pltpu.CompilerParams(vmem_limit_bytes=56 << 20),
        cost_estimate=pl.CostEstimate(
            flops=4 * rows * width * columns,
            bytes_accessed=2 * width * columns + 8 * rows * columns,
            transcendentals=rows * columns,
        ),
        name="head",
    )(place, states, refs, tokens, ref_lse, *heads)


def gather_rows(head_weight):
    half = head_weight.shape[0] // 2
    near = [rotate(head_weight, "y", 1), rotate(head_weight, "y", -1)]
    far = [rotate(near[0][:half], "y", 1), rotate(near[1][half:], "y", -1)]
    return near, far


def swap_cores(head_weight, near, far, after):
    ys, cores = lax.axis_size("y"), lax.axis_size("c")
    y, core = lax.axis_index("y"), lax.axis_index("c")
    late, _ = lax.optimization_barrier((far, after))
    shards, owners = [], []
    for shard, sent, step in (
        ([head_weight], [head_weight], 0),
        (near[:1], near[:1], -1),
        (near[1:], near[1:], 1),
        (far, late, 2),
    ):
        chip = lax.rem(y + step + ys, ys) * cores
        shards += [shard, [rotate(part, "c", 1) for part in sent]]
        owners += [chip + core, chip + 1 - core]
    return shards, owners


def token_columns(head_weight, token_ids, vocab_start):
    depth, vocab_dev = head_weight.shape
    seqs, xs = lax.axis_size(SEQ), lax.axis_size("x")
    rows = token_ids.size
    ids = spread(token_ids.reshape(rows), SEQ).reshape(seqs * rows, 1)
    column = vocab_start + lax.broadcasted_iota(jnp.int32, (1, vocab_dev), 1)
    onehot = (column == ids).astype(jnp.bfloat16)
    found = lax.dot_general(
        head_weight, onehot, (((1,), (1,)), ((), ())), preferred_element_type=jnp.float32
    ).astype(jnp.bfloat16)
    found = found.reshape(xs, depth // xs, seqs, rows).transpose(0, 2, 1, 3)
    found = lax.all_to_all(found, "x", 0, 0)
    found = jnp.sum(found.astype(jnp.float32), axis=0).astype(jnp.bfloat16)
    found = lax.all_to_all(found, "z", 0, 0)
    found = jnp.sum(found.astype(jnp.float32), axis=0).astype(jnp.bfloat16)
    return found


def per_device(hidden, head_weight, ref_logits, token_ids, end_pos, loss_mask, scores):
    batch, segment, width = hidden.shape
    rows = batch * segment
    vocab_dev = head_weight.shape[1]
    seqs, zs, xs = lax.axis_size(SEQ), lax.axis_size("z"), lax.axis_size("x")
    seq_index = lax.axis_index(SEQ)
    seq_start = seq_index * segment
    vocab_start = lax.axis_index(VOC) * vocab_dev

    near, far = gather_rows(head_weight)
    own_columns = token_columns(head_weight, token_ids, vocab_start)
    shards, owners = swap_cores(head_weight, near, far, own_columns)

    refs = ref_logits.reshape(rows, vocab_dev)
    wide = refs.astype(jnp.float32)
    ref_top = jnp.max(wide, axis=1)
    ref_lse = ref_top + jnp.log(jnp.sum(jnp.exp(wide - ref_top[:, None]), axis=1))
    turned_refs = refs.T
    states, turned_refs, own_columns, ref_lse = lax.optimization_barrier(
        (hidden.reshape(rows, width), turned_refs, own_columns, ref_lse)
    )
    pairs = [(i * zs + j, j * zs + i) for i in range(seqs) for j in range(zs)]
    own_columns = lax.ppermute(own_columns, SEQ + ("z",), pairs)
    tokens = token_ids.reshape(rows, 1)
    x_index = lax.axis_index("x")
    logits, stats, *backs, other = run_head(
        states,
        turned_refs,
        (tokens - vocab_start).reshape(1, rows),
        ref_lse[None],
        jnp.stack([x_index] + owners),
        shards,
        xs,
        FIRST,
        lax.axis_size(VOC),
    )
    backs = [part if step == 0 else rotate(part, "x", step) for step, part in enumerate(backs)]
    stats = lax.all_to_all(stats, VOC, 0, 0)
    stats, other = lax.optimization_barrier((stats, other))
    other = lax.all_to_all(other, "z", 0, 0)

    tops = stats[:, 0]
    top_policy = jnp.max(tops, axis=0)
    scale = jnp.exp(tops - top_policy[None])
    total = jnp.sum(stats[:, 1] * scale, axis=0)
    weighted = jnp.sum(stats[:, 2] * scale, axis=0)
    own_logit = jnp.sum(stats[:, 3], axis=0)
    top_ref = jnp.max(stats[:, 4], axis=0)
    lse_ref = top_ref + jnp.log(jnp.sum(jnp.exp(stats[:, 4] - top_ref[None]), axis=0))
    lse_policy = top_policy + jnp.log(total)
    kl_value = (weighted / total - lse_policy + lse_ref).reshape(batch, segment)

    z_index = lax.axis_index("z")
    share = (scale / total[None]).reshape(zs, xs, rows)
    here = lax.dynamic_index_in_dim(share, z_index, 0, keepdims=False)
    back = 0.0
    for step, part in enumerate(backs):
        sender = lax.rem(x_index + xs - step, xs)
        back = back + part.astype(jnp.float32) * lax.dynamic_slice_in_dim(here, sender, 1, 0)
    back = back.astype(jnp.bfloat16).reshape(zs, -1, rows)
    back = lax.all_to_all(back, "z", 0, 0)
    back = jnp.sum(back.astype(jnp.float32), axis=0)

    here = lax.dynamic_index_in_dim(share, x_index, 1, keepdims=True)
    other = jnp.sum(other.astype(jnp.float32) * here, axis=0).astype(jnp.bfloat16)
    other = other.reshape(xs, -1, rows)
    mine = 0.0
    for step in range(xs):
        part = lax.dynamic_index_in_dim(other, lax.rem(x_index + step, xs), 0, keepdims=False)
        mine = mine + (part if step == 0 else rotate(part, "x", step)).astype(jnp.float32)
    back = jnp.concatenate([back, mine], axis=0)

    position = seq_start + lax.broadcasted_iota(jnp.int32, (1, segment), 1)
    live = ((loss_mask == 1) & (position <= end_pos[:, None])).astype(jnp.float32)
    at_end = (position == end_pos[:, None]).astype(jnp.float32)
    reward = -0.01 * kl_value * live + scores[:, None] * at_end
    y, core = lax.axis_index("y"), lax.axis_index("c")
    ys = lax.axis_size("y")
    both = jnp.stack([reward, live])
    both = jnp.stack([both, rotate(both, "c", 1)])
    both = jnp.stack([both] + [rotate(both, "y", step) for step in range(1, ys)])
    both = both.reshape((seqs,) + both.shape[2:])
    rewards, lives = both[:, 0], both[:, 1]
    step = lax.broadcasted_iota(jnp.int32, (seqs, seqs), 0)
    behind = lax.broadcasted_iota(jnp.int32, (seqs, seqs), 1)
    owner, owner_behind = (
        lax.rem(y + ys - at // 2, ys) * 2 + jnp.where(at % 2 == 0, core, 1 - core)
        for at in (step, behind)
    )
    upper = (
        lax.broadcasted_iota(jnp.int32, (segment, segment), 0)
        >= lax.broadcasted_iota(jnp.int32, (segment, segment), 1)
    ).astype(jnp.float32)
    suffix = jnp.dot(
        rewards.reshape(seqs * batch, segment), upper, precision=lax.Precision.HIGHEST
    ).reshape(seqs, batch, segment)
    totals = jnp.sum(rewards, axis=2)
    later = (owner_behind > owner).astype(jnp.float32)[:, :, None]
    carried = jnp.sum(later * totals[None], axis=1)
    returns_all = suffix + carried[:, :, None]
    count = jnp.maximum(jnp.sum(lives), 1.0)
    mean = jnp.sum(lives * returns_all) / count
    var = jnp.sum(lives * returns_all * returns_all) / count - mean * mean
    returns = returns_all[0]
    advantages = (returns - mean) / jnp.sqrt(var + 1e-05)
    factor = (live * advantages / count).reshape(rows)

    prob = jnp.exp(logits - lse_policy[:, None])
    column = vocab_start + lax.broadcasted_iota(jnp.int32, (1, vocab_dev), 1)
    onehot = (column == tokens).astype(jnp.float32)
    logit_grad = (factor[:, None] * (prob - onehot)).astype(jnp.bfloat16)

    own_grad = (factor * (jnp.exp(own_logit - lse_policy) - 1.0)).astype(jnp.bfloat16)
    hidden_grad = factor[None] * back + own_grad.astype(jnp.float32)[None] * own_columns.astype(jnp.float32)
    hidden_grad = hidden_grad.T.reshape(batch, segment, -1).astype(jnp.bfloat16)
    return (logit_grad.reshape(batch, segment, vocab_dev), hidden_grad, advantages)


def solution(mesh):
    chips = mesh.devices.reshape(4, 2, 8, 4)
    fine = Mesh(chips, ("y", "c", "z", "x"))
    in_specs = (
        P(None, SEQ, None),
        P(SEQ, VOC),
        P(None, SEQ, VOC),
        P(None, SEQ),
        P(),
        P(None, SEQ),
        P(),
    )
    out_specs = (P(None, SEQ, VOC), P(None, SEQ, VOC), P(None, SEQ))
    return jax.shard_map(
        per_device, mesh=fine, in_specs=in_specs, out_specs=out_specs, check_vma=False
    )
```

```python
import functools

import jax
import jax.numpy as jnp
from jax import lax
from jax.experimental import pallas as pl
from jax.experimental.pallas import tpu as pltpu
from jax.sharding import Mesh, PartitionSpec as P

SEQ = ("y", "c")
VOC = ("z", "x")
TILE = 128
SUB = 8
WIDE = 8
FIRST = 112


def spread(value, axes):
    count = lax.axis_size(axes)
    return lax.all_to_all(jnp.broadcast_to(value[None], (count,) + value.shape), axes, 0, 0)


def rotate(value, axis, by):
    count = lax.axis_size(axis)
    return lax.ppermute(value, axis, [(i, (i + by) % count) for i in range(count)])


def head_kernel(count, blocks, place_ref, state_hbm, ref_hbm, token_ref, lse_ref, *rest):
    heads, rest = rest[:count], rest[count:]
    logit_hbm, stat_ref, back0, back1, back2, back3, by_block = rest[:7]
    state, refs, head, logit, flipped, turned, result, sems, outsem = rest[7:]
    rows, columns = logit.shape
    width = head.shape[0]
    depth = width // blocks
    backs = (back0, back1, back2, back3)
    parts = len(backs)
    piece = depth // parts
    first = back0.shape[0] // blocks
    edges = list(range(0, columns, WIDE * TILE)) + [columns]
    spans = [slice(low, high) for low, high in zip(edges, edges[1:])]

    get_state = pltpu.make_async_copy(state_hbm, state, outsem.at[0])
    get_refs = pltpu.make_async_copy(ref_hbm, refs, outsem.at[1])

    def fetch(tile):
        copies = []
        for index, part in enumerate(heads):
            place = pl.ds(pl.multiple_of(place_ref[1 + index], SUB * 4), part.shape[0])
            copies.append(
                pltpu.make_async_copy(
                    part.at[:, spans[tile]], head.at[place, spans[tile]], sems.at[tile, index]
                )
            )
            copies[-1].start()
        return copies

    get_state.start()
    copies = [fetch(0), fetch(1)]
    get_state.wait()
    best = jnp.full((SUB, rows), -jnp.inf, jnp.float32)
    for tile, span in enumerate(spans):
        for copy in copies[tile]:
            copy.wait()
        if tile + 2 < len(spans):
            copies.append(fetch(tile + 2))
        if tile + 2 == len(spans):
            get_refs.start()
        values = jnp.dot(state[...], head[:, span], preferred_element_type=jnp.float32)
        logit[:, span] = values
        values = values.T
        flipped[span, :] = values
        best = jnp.maximum(best, jnp.max(values.reshape(-1, SUB, rows), axis=0))
    top = jnp.max(best, axis=0, keepdims=True)
    put_logit = pltpu.make_async_copy(logit, logit_hbm, outsem.at[0])
    put_logit.start()
    get_refs.wait()

    column = lax.broadcasted_iota(jnp.int32, (TILE, rows), 0)

    def fold(terms):
        return jnp.sum(terms.reshape(TILE // SUB, SUB, rows), axis=0)

    def strip(tile, sums):
        span = pl.ds(pl.multiple_of(tile * TILE, TILE), TILE)
        values = flipped[span, :]
        powers = jnp.exp(values - top)
        gap = values - refs[span, :].astype(jnp.float32)
        hit = column == token_ref[...] - tile * TILE
        turned[span, :] = jnp.where(hit, 0.0, powers).astype(jnp.bfloat16)
        return (
            sums[0] + fold(powers),
            sums[1] + fold(powers * gap),
            sums[2] + fold(jnp.where(hit, values, 0.0)),
        )

    zero = jnp.zeros((SUB, rows), jnp.float32)
    sums = lax.fori_loop(0, columns // TILE, strip, (zero, zero, zero))
    total, weighted, own = (jnp.sum(term, axis=0, keepdims=True) for term in sums)
    stats = jnp.concatenate([top, total, weighted, own, lse_ref[...], zero[:3]], axis=0)
    for device in range(stat_ref.shape[0]):
        stat_ref[device] = stats

    place = place_ref[0]

    @pl.loop(0, blocks)
    def _(block):
        span = pl.ds(pl.multiple_of(block * depth, depth), depth)
        result[...] = jnp.dot(
            head[span, :], turned[...], preferred_element_type=jnp.float32
        ).astype(jnp.bfloat16)
        target = pl.ds(pl.multiple_of(block * first, SUB * 2), first)
        for part, back in enumerate(backs):
            source = lax.rem(place + part, parts) * piece
            back[target, :] = result[pl.ds(pl.multiple_of(source, SUB * 4), first), :]
            by_block[block, part * (piece - first) : (part + 1) * (piece - first), :] = result[
                part * piece + first : (part + 1) * piece, :
            ]

    put_logit.wait()

def run_head(states, refs, tokens, ref_lse, place, heads, blocks, parts, first, peers):
    rows, width = states.shape
    columns = heads[0].shape[1]
    vmem = pl.BlockSpec(memory_space=pltpu.VMEM)
    hbm = pl.BlockSpec(memory_space=pl.ANY)
    back = jax.ShapeDtypeStruct((blocks * first, rows), jnp.bfloat16)
    rest = width // blocks - parts * first
    return pl.pallas_call(
        functools.partial(head_kernel, len(heads), blocks),
        out_shape=(
            jax.ShapeDtypeStruct((rows, columns), jnp.float32),
            jax.ShapeDtypeStruct((peers, SUB, rows), jnp.float32),
        ) + (back,) * parts + (jax.ShapeDtypeStruct((blocks, rest, rows), jnp.bfloat16),),
        in_specs=[pl.BlockSpec(memory_space=pltpu.SMEM), hbm, hbm, vmem, vmem] + [hbm] * len(heads),
        out_specs=(hbm,) + (vmem,) * (2 + parts),
        scratch_shapes=[
            pltpu.VMEM((rows, width), jnp.bfloat16),
            pltpu.VMEM((columns, rows), jnp.bfloat16),
            pltpu.VMEM((width, columns), jnp.bfloat16),
            pltpu.VMEM((rows, columns), jnp.float32),
            pltpu.VMEM((columns, rows), jnp.float32),
            pltpu.VMEM((columns, rows), jnp.bfloat16),
            pltpu.VMEM((width // blocks, rows), jnp.bfloat16),
            pltpu.SemaphoreType.DMA((-(-columns // (WIDE * TILE)), len(heads))),
            pltpu.SemaphoreType.DMA((2,)),
        ],
        compiler_params=pltpu.CompilerParams(vmem_limit_bytes=56 << 20),
        cost_estimate=pl.CostEstimate(
            flops=4 * rows * width * columns,
            bytes_accessed=2 * width * columns + 8 * rows * columns,
            transcendentals=rows * columns,
        ),
        name="head",
    )(place, states, refs, tokens, ref_lse, *heads)


def gather_rows(head_weight):
    half = head_weight.shape[0] // 2
    upper, lower = head_weight[:half], head_weight[half:]
    near = [rotate(upper, "y", 1), rotate(lower, "y", -1)]
    late = [rotate(lower, "y", 1), rotate(upper, "y", -1)]
    far = [rotate(near[0], "y", 1), rotate(near[1], "y", -1)]
    own_swap = rotate(head_weight, "c", 1)
    return own_swap, near, list(zip(near + late + far, (-1, 1, -1, 1, 2, 2), (0, half, half, 0, 0, half)))


def swap_cores(head_weight, own_swap, gathered, after):
    depth = head_weight.shape[0]
    ys, cores = lax.axis_size("y"), lax.axis_size("c")
    y, core = lax.axis_index("y"), lax.axis_index("c")
    pieces, starts = [], []
    for piece, step, row in [(head_weight, 0, 0)] + gathered:
        sent = lax.optimization_barrier((piece, after))[0] if step == 2 else piece
        chip = lax.rem(y + step + ys, ys) * cores
        pieces += [piece, own_swap if step == 0 else rotate(sent, "c", 1)]
        starts += [(chip + core) * depth + row, (chip + 1 - core) * depth + row]
    return pieces, starts


def token_columns(head_weight, ids, vocab_start, own_swap, near):
    depth, vocab_dev = head_weight.shape
    seqs, xs = lax.axis_size(SEQ), lax.axis_size("x")
    rows = ids.size // seqs
    column = vocab_start + lax.broadcasted_iota(jnp.int32, (1, vocab_dev), 1)
    onehot = (column == ids).astype(jnp.bfloat16)
    head_weight, _ = lax.optimization_barrier((head_weight, own_swap))
    found = lax.dot_general(
        head_weight, onehot, (((1,), (1,)), ((), ())), preferred_element_type=jnp.float32
    ).astype(jnp.bfloat16)
    found = found.reshape(xs, depth // xs, seqs, rows).transpose(0, 2, 1, 3)
    found, _ = lax.optimization_barrier((found, near))
    found = lax.all_to_all(found, "x", 0, 0)
    found = jnp.sum(found.astype(jnp.float32), axis=0).astype(jnp.bfloat16)
    found = lax.all_to_all(found, "z", 0, 0)
    found = jnp.sum(found.astype(jnp.float32), axis=0).astype(jnp.bfloat16)
    return found


def per_device(hidden, head_weight, ref_logits, token_ids, end_pos, loss_mask, scores):
    batch, segment, width = hidden.shape
    rows = batch * segment
    vocab_dev = head_weight.shape[1]
    seqs, zs, xs = lax.axis_size(SEQ), lax.axis_size("z"), lax.axis_size("x")
    seq_index = lax.axis_index(SEQ)
    seq_start = seq_index * segment
    vocab_start = lax.axis_index(VOC) * vocab_dev

    ids = spread(token_ids.reshape(rows), SEQ).reshape(seqs * rows, 1)
    own_swap, near, gathered = gather_rows(head_weight)
    own_columns = token_columns(head_weight, ids, vocab_start, own_swap, near)
    pieces, starts = swap_cores(head_weight, own_swap, gathered, own_columns)

    refs = ref_logits.reshape(rows, vocab_dev)
    wide = refs.astype(jnp.float32)
    ref_top = jnp.max(wide, axis=1)
    ref_lse = ref_top + jnp.log(jnp.sum(jnp.exp(wide - ref_top[:, None]), axis=1))
    turned_refs = refs.T
    states, turned_refs, own_columns, ref_lse = lax.optimization_barrier(
        (hidden.reshape(rows, width), turned_refs, own_columns, ref_lse)
    )
    pairs = [(i * zs + j, j * zs + i) for i in range(seqs) for j in range(zs)]
    own_columns = lax.ppermute(own_columns, SEQ + ("z",), pairs)
    tokens = token_ids.reshape(rows, 1)
    x_index = lax.axis_index("x")
    logits, stats, *backs, other = run_head(
        states,
        turned_refs,
        (tokens - vocab_start).reshape(1, rows),
        ref_lse[None],
        jnp.stack([x_index] + starts),
        pieces,
        seqs,
        xs,
        FIRST,
        lax.axis_size(VOC),
    )
    backs = [part if step == 0 else rotate(part, "x", step) for step, part in enumerate(backs)]
    stats = lax.all_to_all(stats, VOC, 0, 0)
    stats, other = lax.optimization_barrier((stats, other))
    other = lax.all_to_all(other, "z", 0, 0)

    tops = stats[:, 0]
    top_policy = jnp.max(tops, axis=0)
    scale = jnp.exp(tops - top_policy[None])
    total = jnp.sum(stats[:, 1] * scale, axis=0)
    weighted = jnp.sum(stats[:, 2] * scale, axis=0)
    own_logit = jnp.sum(stats[:, 3], axis=0)
    top_ref = jnp.max(stats[:, 4], axis=0)
    lse_ref = top_ref + jnp.log(jnp.sum(jnp.exp(stats[:, 4] - top_ref[None]), axis=0))
    lse_policy = top_policy + jnp.log(total)
    kl_value = (weighted / total - lse_policy + lse_ref).reshape(batch, segment)

    z_index = lax.axis_index("z")
    share = (scale / total[None]).reshape(zs, xs, rows)
    here = lax.dynamic_index_in_dim(share, z_index, 0, keepdims=False)
    back = 0.0
    for step, part in enumerate(backs):
        sender = lax.rem(x_index + xs - step, xs)
        back = back + part.astype(jnp.float32) * lax.dynamic_slice_in_dim(here, sender, 1, 0)
    back = back.astype(jnp.bfloat16).reshape(zs, -1, rows)
    back = lax.all_to_all(back, "z", 0, 0)
    back = jnp.sum(back.astype(jnp.float32), axis=0)

    here = lax.dynamic_index_in_dim(share, x_index, 1, keepdims=True)
    other = jnp.sum(other.astype(jnp.float32) * here, axis=0).astype(jnp.bfloat16)
    other = other.reshape(xs, -1, rows)
    mine = 0.0
    for step in range(xs):
        part = lax.dynamic_index_in_dim(other, lax.rem(x_index + step, xs), 0, keepdims=False)
        mine = mine + (part if step == 0 else rotate(part, "x", step)).astype(jnp.float32)
    back = jnp.concatenate([back, mine], axis=0)

    position = seq_start + lax.broadcasted_iota(jnp.int32, (1, segment), 1)
    live = ((loss_mask == 1) & (position <= end_pos[:, None])).astype(jnp.float32)
    at_end = (position == end_pos[:, None]).astype(jnp.float32)
    reward = -0.01 * kl_value * live + scores[:, None] * at_end
    y, core = lax.axis_index("y"), lax.axis_index("c")
    ys = lax.axis_size("y")
    both = jnp.stack([reward, live])
    both = jnp.stack([both, rotate(both, "c", 1)])
    both = jnp.stack([both] + [rotate(both, "y", step) for step in range(1, ys)])
    both = both.reshape((seqs,) + both.shape[2:])
    rewards, lives = both[:, 0], both[:, 1]
    step = lax.broadcasted_iota(jnp.int32, (seqs, seqs), 0)
    behind = lax.broadcasted_iota(jnp.int32, (seqs, seqs), 1)
    owner, owner_behind = (
        lax.rem(y + ys - at // 2, ys) * 2 + jnp.where(at % 2 == 0, core, 1 - core)
        for at in (step, behind)
    )
    upper = (
        lax.broadcasted_iota(jnp.int32, (segment, segment), 0)
        >= lax.broadcasted_iota(jnp.int32, (segment, segment), 1)
    ).astype(jnp.float32)
    suffix = jnp.dot(
        rewards.reshape(seqs * batch, segment), upper, precision=lax.Precision.HIGHEST
    ).reshape(seqs, batch, segment)
    totals = jnp.sum(rewards, axis=2)
    later = (owner_behind > owner).astype(jnp.float32)[:, :, None]
    carried = jnp.sum(later * totals[None], axis=1)
    returns_all = suffix + carried[:, :, None]
    count = jnp.maximum(jnp.sum(lives), 1.0)
    mean = jnp.sum(lives * returns_all) / count
    var = jnp.sum(lives * returns_all * returns_all) / count - mean * mean
    returns = returns_all[0]
    advantages = (returns - mean) / jnp.sqrt(var + 1e-05)
    factor = (live * advantages / count).reshape(rows)

    prob = jnp.exp(logits - lse_policy[:, None])
    column = vocab_start + lax.broadcasted_iota(jnp.int32, (1, vocab_dev), 1)
    onehot = (column == tokens).astype(jnp.float32)
    logit_grad = (factor[:, None] * (prob - onehot)).astype(jnp.bfloat16)

    own_grad = (factor * (jnp.exp(own_logit - lse_policy) - 1.0)).astype(jnp.bfloat16)
    hidden_grad = factor[None] * back + own_grad.astype(jnp.float32)[None] * own_columns.astype(jnp.float32)
    hidden_grad = hidden_grad.T.reshape(batch, segment, -1).astype(jnp.bfloat16)
    return (logit_grad.reshape(batch, segment, vocab_dev), hidden_grad, advantages)


def solution(mesh):
    chips = mesh.devices.reshape(4, 2, 8, 4)
    fine = Mesh(chips, ("y", "c", "z", "x"))
    in_specs = (
        P(None, SEQ, None),
        P(SEQ, VOC),
        P(None, SEQ, VOC),
        P(None, SEQ),
        P(),
        P(None, SEQ),
        P(),
    )
    out_specs = (P(None, SEQ, VOC), P(None, SEQ, VOC), P(None, SEQ))
    return jax.shard_map(
        per_device, mesh=fine, in_specs=in_specs, out_specs=out_specs, check_vma=False
    )
```

```python
import functools

import jax
import jax.numpy as jnp
from jax import lax
from jax.experimental import pallas as pl
from jax.experimental.pallas import tpu as pltpu
from jax.sharding import Mesh, PartitionSpec as P

SEQ = ("y", "c")
VOC = ("z", "x")
TILE = 128
SUB = 8
WIDE = 8
FIRST = 112


def spread(value, axes):
    count = lax.axis_size(axes)
    return lax.all_to_all(jnp.broadcast_to(value[None], (count,) + value.shape), axes, 0, 0)


def rotate(value, axis, by):
    count = lax.axis_size(axis)
    return lax.ppermute(value, axis, [(i, (i + by) % count) for i in range(count)])


def head_kernel(count, blocks, place_ref, state_hbm, ref_hbm, token_ref, lse_ref, *rest):
    heads, rest = rest[:count], rest[count:]
    logit_hbm, stat_ref, back0, back1, back2, back3, by_block = rest[:7]
    state, refs, head, logit, flipped, turned, result, sems, outsem = rest[7:]
    rows, columns = logit.shape
    width = head.shape[0]
    depth = width // blocks
    backs = (back0, back1, back2, back3)
    parts = len(backs)
    piece = depth // parts
    first = back0.shape[0] // blocks
    edges = list(range(0, columns, WIDE * TILE)) + [columns]
    spans = [slice(low, high) for low, high in zip(edges, edges[1:])]

    get_state = pltpu.make_async_copy(state_hbm, state, outsem.at[0])
    get_refs = pltpu.make_async_copy(ref_hbm, refs, outsem.at[1])

    def fetch(tile):
        copies = []
        for index, part in enumerate(heads):
            place = pl.ds(pl.multiple_of(place_ref[1 + index], SUB * 4), part.shape[0])
            copies.append(
                pltpu.make_async_copy(
                    part.at[:, spans[tile]], head.at[place, spans[tile]], sems.at[tile, index]
                )
            )
            copies[-1].start()
        return copies

    get_state.start()
    copies = [fetch(0), fetch(1)]
    get_state.wait()
    best = jnp.full((SUB, rows), -jnp.inf, jnp.float32)
    for tile, span in enumerate(spans):
        for copy in copies[tile]:
            copy.wait()
        if tile + 2 < len(spans):
            copies.append(fetch(tile + 2))
        if tile + 2 == len(spans):
            get_refs.start()
        values = jnp.dot(state[...], head[:, span], preferred_element_type=jnp.float32)
        logit[:, span] = values
        values = values.T
        flipped[span, :] = values
        best = jnp.maximum(best, jnp.max(values.reshape(-1, SUB, rows), axis=0))
    top = jnp.max(best, axis=0, keepdims=True)
    put_logit = pltpu.make_async_copy(logit, logit_hbm, outsem.at[0])
    put_logit.start()
    get_refs.wait()

    column = lax.broadcasted_iota(jnp.int32, (TILE, rows), 0)

    def fold(terms):
        return jnp.sum(terms.reshape(TILE // SUB, SUB, rows), axis=0)

    def strip(tile, sums):
        span = pl.ds(pl.multiple_of(tile * TILE, TILE), TILE)
        values = flipped[span, :]
        powers = jnp.exp(values - top)
        gap = values - refs[span, :].astype(jnp.float32)
        hit = column == token_ref[...] - tile * TILE
        turned[span, :] = jnp.where(hit, 0.0, powers).astype(jnp.bfloat16)
        return (
            sums[0] + fold(powers),
            sums[1] + fold(powers * gap),
            sums[2] + fold(jnp.where(hit, values, 0.0)),
        )

    zero = jnp.zeros((SUB, rows), jnp.float32)
    sums = lax.fori_loop(0, columns // TILE, strip, (zero, zero, zero))
    total, weighted, own = (jnp.sum(term, axis=0, keepdims=True) for term in sums)
    stats = jnp.concatenate([top, total, weighted, own, lse_ref[...], zero[:3]], axis=0)
    for device in range(stat_ref.shape[0]):
        stat_ref[device] = stats

    place = place_ref[0]

    @pl.loop(0, blocks)
    def _(block):
        span = pl.ds(pl.multiple_of(block * depth, depth), depth)
        result[...] = jnp.dot(
            head[span, :], turned[...], preferred_element_type=jnp.float32
        ).astype(jnp.bfloat16)
        target = pl.ds(pl.multiple_of(block * first, SUB * 2), first)
        for part, back in enumerate(backs):
            source = lax.rem(place + part, parts) * piece
            back[target, :] = result[pl.ds(pl.multiple_of(source, SUB * 4), first), :]
            by_block[block, part * (piece - first) : (part + 1) * (piece - first), :] = result[
                part * piece + first : (part + 1) * piece, :
            ]

    put_logit.wait()

def run_head(states, refs, tokens, ref_lse, place, heads, blocks, parts, first, peers):
    rows, width = states.shape
    columns = heads[0].shape[1]
    vmem = pl.BlockSpec(memory_space=pltpu.VMEM)
    hbm = pl.BlockSpec(memory_space=pl.ANY)
    back = jax.ShapeDtypeStruct((blocks * first, rows), jnp.bfloat16)
    rest = width // blocks - parts * first
    return pl.pallas_call(
        functools.partial(head_kernel, len(heads), blocks),
        out_shape=(
            jax.ShapeDtypeStruct((rows, columns), jnp.float32),
            jax.ShapeDtypeStruct((peers, SUB, rows), jnp.float32),
        ) + (back,) * parts + (jax.ShapeDtypeStruct((blocks, rest, rows), jnp.bfloat16),),
        in_specs=[pl.BlockSpec(memory_space=pltpu.SMEM), hbm, hbm, vmem, vmem] + [hbm] * len(heads),
        out_specs=(hbm,) + (vmem,) * (2 + parts),
        scratch_shapes=[
            pltpu.VMEM((rows, width), jnp.bfloat16),
            pltpu.VMEM((columns, rows), jnp.bfloat16),
            pltpu.VMEM((width, columns), jnp.bfloat16),
            pltpu.VMEM((rows, columns), jnp.float32),
            pltpu.VMEM((columns, rows), jnp.float32),
            pltpu.VMEM((columns, rows), jnp.bfloat16),
            pltpu.VMEM((width // blocks, rows), jnp.bfloat16),
            pltpu.SemaphoreType.DMA((-(-columns // (WIDE * TILE)), len(heads))),
            pltpu.SemaphoreType.DMA((2,)),
        ],
        compiler_params=pltpu.CompilerParams(vmem_limit_bytes=56 << 20),
        cost_estimate=pl.CostEstimate(
            flops=4 * rows * width * columns,
            bytes_accessed=2 * width * columns + 8 * rows * columns,
            transcendentals=rows * columns,
        ),
        name="head",
    )(place, states, refs, tokens, ref_lse, *heads)


def gather_rows(head_weight):
    half = head_weight.shape[0] // 2
    upper, lower = head_weight[:half], head_weight[half:]
    near = [rotate(upper, "y", 1), rotate(lower, "y", -1)]
    late = [rotate(lower, "y", 1), rotate(upper, "y", -1)]
    far = [rotate(near[0], "y", 1), rotate(near[1], "y", -1)]
    own_swap = rotate(head_weight, "c", 1)
    return own_swap, near, list(zip(near + late + far, (-1, 1, -1, 1, 2, 2), (0, half, half, 0, 0, half)))


def swap_cores(head_weight, own_swap, gathered, after):
    depth = head_weight.shape[0]
    ys, cores = lax.axis_size("y"), lax.axis_size("c")
    y, core = lax.axis_index("y"), lax.axis_index("c")
    pieces, starts = [], []
    for piece, step, row in [(head_weight, 0, 0)] + gathered:
        sent = lax.optimization_barrier((piece, after))[0] if step == 2 else piece
        chip = lax.rem(y + step + ys, ys) * cores
        pieces += [piece, own_swap if step == 0 else rotate(sent, "c", 1)]
        starts += [(chip + core) * depth + row, (chip + 1 - core) * depth + row]
    return pieces, starts


def token_columns(head_weight, ids, vocab_start, own_swap, near):
    depth, vocab_dev = head_weight.shape
    seqs, xs = lax.axis_size(SEQ), lax.axis_size("x")
    rows = ids.size // seqs
    column = vocab_start + lax.broadcasted_iota(jnp.int32, (1, vocab_dev), 1)
    onehot = (column == ids).astype(jnp.bfloat16)
    head_weight, _ = lax.optimization_barrier((head_weight, own_swap))
    found = lax.dot_general(
        head_weight, onehot, (((1,), (1,)), ((), ())), preferred_element_type=jnp.float32
    ).astype(jnp.bfloat16)
    found = found.reshape(xs, depth // xs, seqs, rows).transpose(0, 2, 1, 3)
    found, _ = lax.optimization_barrier((found, near))
    found = lax.all_to_all(found, "x", 0, 0)
    found = jnp.sum(found.astype(jnp.float32), axis=0).astype(jnp.bfloat16)
    found = lax.all_to_all(found, "z", 0, 0)
    found = jnp.sum(found.astype(jnp.float32), axis=0).astype(jnp.bfloat16)
    return found


def per_device(hidden, head_weight, ref_logits, token_ids, end_pos, loss_mask, scores):
    batch, segment, width = hidden.shape
    rows = batch * segment
    vocab_dev = head_weight.shape[1]
    seqs, zs, xs = lax.axis_size(SEQ), lax.axis_size("z"), lax.axis_size("x")
    seq_index = lax.axis_index(SEQ)
    seq_start = seq_index * segment
    vocab_start = lax.axis_index(VOC) * vocab_dev

    ids = spread(token_ids.reshape(rows), SEQ).reshape(seqs * rows, 1)
    own_swap, near, gathered = gather_rows(head_weight)
    own_columns = token_columns(head_weight, ids, vocab_start, own_swap, near)
    pieces, starts = swap_cores(head_weight, own_swap, gathered, own_columns)

    refs = ref_logits.reshape(rows, vocab_dev)
    wide = refs.astype(jnp.float32)
    ref_top = jnp.max(wide, axis=1)
    ref_lse = ref_top + jnp.log(jnp.sum(jnp.exp(wide - ref_top[:, None]), axis=1))
    turned_refs = refs.T
    states, turned_refs, own_columns, ref_lse = lax.optimization_barrier(
        (hidden.reshape(rows, width), turned_refs, own_columns, ref_lse)
    )
    pairs = [(i * zs + j, j * zs + i) for i in range(seqs) for j in range(zs)]
    tokens = token_ids.reshape(rows, 1)
    x_index = lax.axis_index("x")
    logits, stats, *backs, other = run_head(
        states,
        turned_refs,
        (tokens - vocab_start).reshape(1, rows),
        ref_lse[None],
        jnp.stack([x_index] + starts),
        pieces,
        seqs,
        xs,
        FIRST,
        lax.axis_size(VOC),
    )
    backs = [part if step == 0 else rotate(part, "x", step) for step, part in enumerate(backs)]
    stats = lax.all_to_all(stats, VOC, 0, 0)
    stats, other = lax.optimization_barrier((stats, other))
    other = lax.all_to_all(other, "z", 0, 0)

    tops = stats[:, 0]
    top_policy = jnp.max(tops, axis=0)
    scale = jnp.exp(tops - top_policy[None])
    total = jnp.sum(stats[:, 1] * scale, axis=0)
    weighted = jnp.sum(stats[:, 2] * scale, axis=0)
    own_logit = jnp.sum(stats[:, 3], axis=0)
    top_ref = jnp.max(stats[:, 4], axis=0)
    lse_ref = top_ref + jnp.log(jnp.sum(jnp.exp(stats[:, 4] - top_ref[None]), axis=0))
    lse_policy = top_policy + jnp.log(total)
    kl_value = (weighted / total - lse_policy + lse_ref).reshape(batch, segment)
    own_columns, kl_value = lax.optimization_barrier((own_columns, kl_value))
    own_columns = lax.ppermute(own_columns, SEQ + ("z",), pairs)

    z_index = lax.axis_index("z")
    share = (scale / total[None]).reshape(zs, xs, rows)
    here = lax.dynamic_index_in_dim(share, z_index, 0, keepdims=False)
    back = 0.0
    for step, part in enumerate(backs):
        sender = lax.rem(x_index + xs - step, xs)
        back = back + part.astype(jnp.float32) * lax.dynamic_slice_in_dim(here, sender, 1, 0)
    back = back.astype(jnp.bfloat16).reshape(zs, -1, rows)
    back = lax.all_to_all(back, "z", 0, 0)
    back = jnp.sum(back.astype(jnp.float32), axis=0)

    here = lax.dynamic_index_in_dim(share, x_index, 1, keepdims=True)
    other = jnp.sum(other.astype(jnp.float32) * here, axis=0).astype(jnp.bfloat16)
    other = other.reshape(xs, -1, rows)
    mine = 0.0
    for step in range(xs):
        part = lax.dynamic_index_in_dim(other, lax.rem(x_index + step, xs), 0, keepdims=False)
        mine = mine + (part if step == 0 else rotate(part, "x", step)).astype(jnp.float32)
    back = jnp.concatenate([back, mine], axis=0)

    position = seq_start + lax.broadcasted_iota(jnp.int32, (1, segment), 1)
    live = ((loss_mask == 1) & (position <= end_pos[:, None])).astype(jnp.float32)
    at_end = (position == end_pos[:, None]).astype(jnp.float32)
    reward = -0.01 * kl_value * live + scores[:, None] * at_end
    y, core = lax.axis_index("y"), lax.axis_index("c")
    ys = lax.axis_size("y")
    both = jnp.stack([reward, live])
    both = jnp.stack([both, rotate(both, "c", 1)])
    both = both[None]
    for reach in (1, 2):
        both = jnp.concatenate([both, rotate(both, "y", reach)])
    both = both.reshape((seqs,) + both.shape[2:])
    rewards, lives = both[:, 0], both[:, 1]
    step = lax.broadcasted_iota(jnp.int32, (seqs, seqs), 0)
    behind = lax.broadcasted_iota(jnp.int32, (seqs, seqs), 1)
    owner, owner_behind = (
        lax.rem(y + ys - at // 2, ys) * 2 + jnp.where(at % 2 == 0, core, 1 - core)
        for at in (step, behind)
    )
    upper = (
        lax.broadcasted_iota(jnp.int32, (segment, segment), 0)
        >= lax.broadcasted_iota(jnp.int32, (segment, segment), 1)
    ).astype(jnp.float32)
    suffix = jnp.dot(
        rewards.reshape(seqs * batch, segment), upper, precision=lax.Precision.HIGHEST
    ).reshape(seqs, batch, segment)
    totals = jnp.sum(rewards, axis=2)
    later = (owner_behind > owner).astype(jnp.float32)[:, :, None]
    carried = jnp.sum(later * totals[None], axis=1)
    returns_all = suffix + carried[:, :, None]
    count = jnp.maximum(jnp.sum(lives), 1.0)
    mean = jnp.sum(lives * returns_all) / count
    var = jnp.sum(lives * returns_all * returns_all) / count - mean * mean
    returns = returns_all[0]
    advantages = (returns - mean) / jnp.sqrt(var + 1e-05)
    factor = (live * advantages / count).reshape(rows)

    prob = jnp.exp(logits - lse_policy[:, None])
    column = vocab_start + lax.broadcasted_iota(jnp.int32, (1, vocab_dev), 1)
    onehot = (column == tokens).astype(jnp.float32)
    logit_grad = (factor[:, None] * (prob - onehot)).astype(jnp.bfloat16)

    own_grad = (factor * (jnp.exp(own_logit - lse_policy) - 1.0)).astype(jnp.bfloat16)
    hidden_grad = factor[None] * back + own_grad.astype(jnp.float32)[None] * own_columns.astype(jnp.float32)
    hidden_grad = hidden_grad.T.reshape(batch, segment, -1).astype(jnp.bfloat16)
    return (logit_grad.reshape(batch, segment, vocab_dev), hidden_grad, advantages)


def solution(mesh):
    chips = mesh.devices.reshape(4, 2, 8, 4)
    fine = Mesh(chips, ("y", "c", "z", "x"))
    in_specs = (
        P(None, SEQ, None),
        P(SEQ, VOC),
        P(None, SEQ, VOC),
        P(None, SEQ),
        P(),
        P(None, SEQ),
        P(),
    )
    out_specs = (P(None, SEQ, VOC), P(None, SEQ, VOC), P(None, SEQ))
    return jax.shard_map(
        per_device, mesh=fine, in_specs=in_specs, out_specs=out_specs, check_vma=False
    )
```
